256 devices in a mesh: rows: 8 (over x, core), cols: 32 (over z, y).
Axes of the slice: x: 4, y: 4, z: 8, core: 2. Of those that a mesh axis runs over, the one named last changes fastest.
Arguments:
- video: bfloat16 [1920, 256, 128], P('cols', 'rows'), may hold values from -8 to 8, as said below
- fore_prev: float32 [1920, 256, 128], P('cols', 'rows'), may hold values from -4 to 4
- mult: float32 [1920, 256, 128], P('cols', 'rows'), may hold values from -4 to 4
- dual_tv: float32 [3, 1920, 256, 128], P(None, 'cols', 'rows'), may hold values from -1 to 1
- shrink: float32 [2], replicated, may hold values from 0.3 to 3
- tv_weight: float32 [2], replicated, may hold values from 0.3 to 1.5
Outputs:
- low_rank: float32 [1920, 256, 128], P('cols', 'rows')
- fore: float32 [1920, 256, 128], P('cols', 'rows')
- mult_out: float32 [1920, 256, 128], P('cols', 'rows')
- dual_out: float32 [3, 1920, 256, 128], P(None, 'cols', 'rows')
The draws below stay inside these ranges and needn't reach their ends.
Inputs may be any that keep to these rules, and one draw needn't show every extreme that they name: `video`: pixel values.
All inputs are finite; a program needn't handle non-finite values.
Results may differ from the reference program's by a relative error of at most 0.0003.
Values sent between devices are 32-bit elements; how exact they have to be, the bound alone decides.
No kernel may reach another device: no remote copies, remote signals or barrier semaphores. Data moves between devices by JAX's collectives and lax.ppermute only.
A program may use at most 64 MiB of HBM per device.

```python
import math
import jax
import jax.numpy as jnp
from jax import lax

CAMS = 2
F = 64
WIDTH = 1920
TV_STEPS = 4
H = 256


def draw_video(key, part):
    keys = jax.random.split(key, 3)
    comps = 6
    coef = jax.random.normal(keys[0], (CAMS, comps, F), jnp.float32)
    spatial = jax.random.normal(keys[1], (CAMS, comps, H, WIDTH), jnp.float32)
    colpos = jnp.arange(WIDTH, dtype=jnp.float32) / WIDTH
    rowpos = jnp.arange(H, dtype=jnp.float32) / H
    noise = 0.5 * jax.random.normal(keys[2], (CAMS, F, H, WIDTH), jnp.float32)
    total = jnp.zeros((CAMS, F, H, WIDTH), jnp.float32)
    for index in range(comps):
        across = colpos if index % 2 == 0 else 1.0 - colpos
        downward = rowpos if index % 3 == 0 else 1.0 - rowpos
        envelope = 10.0 ** (across[None, :] + 0.5 * downward[:, None] - 0.9)
        total = total + coef[:, index, :, None, None] * (spatial[:, index] * envelope[None])[:, None]
    result = jnp.clip(0.45 * total + noise, -8.0, 8.0)
    result = jnp.transpose(result, (3, 2, 0, 1)).reshape(WIDTH, H, CAMS * F)
    return result.astype(jnp.bfloat16)


def block_levels(rng, extent, pieces, least, top_value):
    level, own = 1.0, jax.random.fold_in(rng, 6)
    for axis_at, blocks in pieces:
        draws = jnp.exp(jax.random.uniform(jax.random.fold_in(own, axis_at), (blocks,), jnp.float32, least / len(pieces), top_value / len(pieces)))
        level = level * jnp.repeat(draws, extent[axis_at] // blocks).reshape([-1 if axis == axis_at else 1 for axis in range(len(extent))])
    return level


def normal_values(rng, shape, scale, reach, shards=(), kind=jnp.bfloat16):
    loudness = block_levels(rng, shape, shards, -0.22, 0.18) if shards else 1.0
    drawn = jax.random.normal(rng, shape, jnp.float32) * scale * loudness
    return jnp.minimum(jnp.maximum(drawn, -reach), reach).astype(kind)


def setup_inputs(seed: int = 0) -> dict:
    streams_of = jax.random.split(jax.random.key(seed), 7)
    return {
        "video": draw_video(jax.random.fold_in(streams_of[6], 71), 0),
        "fore_prev": normal_values(streams_of[1], (WIDTH, H, CAMS * F), 0.5, 4.0, ((0, 32), (1, 8)), jnp.float32),
        "mult": normal_values(streams_of[2], (WIDTH, H, CAMS * F), 0.5, 4.0, ((0, 32), (1, 8)), jnp.float32),
        "dual_tv": jnp.clip(jax.random.uniform(streams_of[3], (3, WIDTH, H, CAMS * F), jnp.float32, -1.0, 1.0) * block_levels(streams_of[3], (3, WIDTH, H, CAMS * F), ((1, 32), (2, 8)), -0.4, 0.0), -1.0, 1.0),
        "shrink": jnp.clip(jnp.exp(jax.random.uniform(streams_of[4], (CAMS,), jnp.float32, math.log(0.3), math.log(3.0))), 0.3, 3.0),
        "tv_weight": jnp.clip(jnp.exp(jax.random.uniform(streams_of[5], (CAMS,), jnp.float32, math.log(0.3), math.log(1.5))), 0.3, 1.5),
    }


MU = 1.25
KAPPA = 0.08

def prev_local(field, axis):
    count = field.shape[axis]
    zeros = jnp.zeros_like(lax.slice_in_dim(field, 0, 1, axis=axis))
    return jnp.concatenate([zeros, lax.slice_in_dim(field, 0, count - 1, axis=axis)], axis)

def next_local(field, axis):
    count = field.shape[axis]
    zeros = jnp.zeros_like(lax.slice_in_dim(field, 0, 1, axis=axis))
    return jnp.concatenate([lax.slice_in_dim(field, 1, count, axis=axis), zeros], axis)

def shrink_filter(gram, shrink):
    frames = gram.shape[-1]
    trace = jnp.trace(gram, axis1=1, axis2=2)
    tau = shrink * trace / frames
    shifted = gram + tau[:, None, None] * jnp.eye(frames, dtype=gram.dtype)[None]
    factor = jnp.linalg.cholesky(shifted)
    return jax.vmap(lambda lower, right: jax.scipy.linalg.cho_solve((lower, True), right))(factor, gram)

def divergence(p_f, p_h, p_w, masks):
    mask_f, mask_h, mask_w = masks
    q_f = p_f * mask_f
    q_h = p_h * mask_h
    q_w = p_w * mask_w
    return q_f - prev_local(q_f, 2) + (q_h - prev_local(q_h, 1)) + (q_w - prev_local(q_w, 0))

def gradient(field, masks):
    mask_f, mask_h, mask_w = masks
    return ((next_local(field, 2) - field) * mask_f, (next_local(field, 1) - field) * mask_h, (next_local(field, 0) - field) * mask_w)

def reference(video, fore_prev, mult, dual_tv, shrink, tv_weight):
    frames = video.astype(jnp.float32)
    data = frames - fore_prev + mult / MU
    count_w, count_h, merged = data.shape
    cams = shrink.shape[0]
    count_f = merged // cams
    flat = data.reshape(count_w * count_h, cams, count_f)
    gram = jnp.einsum('pcf,pcg->cfg', flat, flat, precision=lax.Precision.HIGHEST)
    filt = shrink_filter(gram, shrink)
    low_rank = jnp.einsum('pcg,cgf->pcf', flat, filt, precision=lax.Precision.HIGHEST).reshape(count_w, count_h, merged)
    target = frames - low_rank + mult / MU
    mask_f = (jnp.arange(merged) % count_f < count_f - 1).astype(jnp.float32)[None, None, :]
    mask_h = (jnp.arange(count_h) < count_h - 1).astype(jnp.float32)[None, :, None]
    mask_w = (jnp.arange(count_w) < count_w - 1).astype(jnp.float32)[:, None, None]
    masks = (mask_f, mask_h, mask_w)
    lam = jnp.repeat(tv_weight, count_f)[None, None, :]
    p_f, p_h, p_w = (dual_tv[0], dual_tv[1], dual_tv[2])
    for step in range(TV_STEPS):
        field = target - lam * divergence(p_f, p_h, p_w, masks)
        g_f, g_h, g_w = gradient(field, masks)
        p_f = jnp.clip(p_f + KAPPA / lam * g_f, -1.0, 1.0)
        p_h = jnp.clip(p_h + KAPPA / lam * g_h, -1.0, 1.0)
        p_w = jnp.clip(p_w + KAPPA / lam * g_w, -1.0, 1.0)
    fore = target - lam * divergence(p_f, p_h, p_w, masks)
    mult_out = mult + MU * (frames - low_rank - fore)
    return (low_rank, fore, mult_out, jnp.stack([p_f, p_h, p_w]))
```

```python
import jax
import jax.numpy as jnp
from jax import lax
from jax.experimental import pallas as pl
from jax.experimental.pallas import tpu as pltpu
from jax.sharding import PartitionSpec as P


TV_STEPS = 4
MU = 1.25
KAPPA = 0.08
M = 4
CORES = 2
GROUPS = 6
NY = 4
INTERPRET = False


def ring_rounds(n):
    if n == 1:
        return []
    if n == 2:
        return [[1, 0]]
    even = [i ^ 1 for i in range(n)]
    odd = [(i + 1) % n if i % 2 else (i - 1) % n for i in range(n)]
    if n == 4:
        return [even, odd]
    assert n == 8
    return [even, odd, [3, 6, 5, 0, 7, 2, 1, 4]]


def reduction_rounds(rows, cols):
    nx, nz = rows // CORES, cols // NY
    out = [("rows", [r ^ 1 for r in range(rows)])]
    for to in ring_rounds(nz):
        out.append(("cols", [to[c // NY] * NY + c % NY for c in range(cols)]))
    for to in ring_rounds(NY):
        out.append(("cols", [c // NY * NY + to[c % NY] for c in range(cols)]))
    for to in ring_rounds(nx):
        out.append(("rows", [to[r // CORES] * CORES + r % CORES for r in range(rows)]))
    return out


def iota(shape, dim):
    return lax.broadcasted_iota(jnp.int32, shape, dim)


def split(x):
    hi = x.astype(jnp.bfloat16)
    return hi, (x - hi.astype(jnp.float32)).astype(jnp.bfloat16)


def pre_kernel(lam_ref, video, fore, mult, dual, gram, data, base, row_lo, row_hi, col_lo, col_hi):
    tw, th, n = data.shape
    half = n // 2
    step = 4
    zero = jnp.zeros((n, 2 * n), jnp.float32)

    def chunk(i, acc):
        at = pl.ds(i * step, step)
        b = video[at].astype(jnp.float32) + mult[at] * (1.0 / MU)
        d = b - fore[at]
        base[at] = b
        data[at] = d
        row_hi[0, at] = d[:, :M]
        row_lo[0, at] = d[:, th - M :]
        row_hi[1, at] = b[:, :M]
        row_lo[1, at] = b[:, th - M :]
        for k in range(3):
            row_hi[2 + k, at] = dual[k, at, :M]
            row_lo[2 + k, at] = dual[k, at, th - M :]
        hi, lo = split(d.reshape(step * th, n))
        return acc + lax.dot_general(
            hi, jnp.concatenate([hi, lo], 1), (((0,), (0,)), ((), ())), preferred_element_type=jnp.float32
        )

    acc = lax.fori_loop(0, tw // step, chunk, zero)
    lane = iota((1, n), 1)
    lam = jnp.where(lane < half, lam_ref[0], lam_ref[1])
    row_lo[1, :, 0:1, :] = row_lo[1, :, 0:1, :] + lam[None] * dual[1, :, th - M - 1 : th - M, :]
    col_hi[0] = data[:M]
    col_lo[0] = data[tw - M :]
    col_hi[1] = base[:M]
    col_lo[1] = base[tw - M :]
    for k in range(3):
        col_hi[2 + k] = dual[k, :M]
        col_lo[2 + k] = dual[k, tw - M :]
    col_lo[1, 0] = base[tw - M] + lam * dual[2, tw - M - 1]
    cross0, cross1 = acc[:half, n:], acc[half:, n:]
    i, j = iota((half, n), 0), iota((half, n), 1)
    cross = jnp.where(j < half, cross0, cross1)
    whole = jnp.where(j < half, acc[:half, :n], acc[half:, :n]) + cross
    turned = jnp.concatenate([cross[:, :half].T, cross[:, half:].T], 1)
    whole = whole + turned
    other = pltpu.roll(whole, half, 1)
    packed = jnp.where(i <= j, whole, other)
    diag = jnp.sum(jnp.where(i == j, other, 0.0), 0, keepdims=True)
    quarter = half // 2
    gram[:quarter] = jnp.where(j[:quarter] < half, packed[:quarter], pltpu.roll(packed[quarter:], half, 1))
    gram[quarter:] = jnp.broadcast_to(diag, (8, n))


def pre(lam, video, fore, mult, dual):
    tw, th, n = fore.shape
    f32 = lambda *s: jax.ShapeDtypeStruct(s, jnp.float32)
    vmem = pl.BlockSpec(memory_space=pltpu.VMEM)
    return pl.pallas_call(
        pre_kernel,
        out_shape=(
            f32(n // 4 + 8, n),
            f32(tw, th, n),
            f32(tw, th, n),
            f32(5, tw, M, n),
            f32(5, tw, M, n),
            f32(5, M, th, n),
            f32(5, M, th, n),
        ),
        in_specs=[pl.BlockSpec(memory_space=pltpu.SMEM)] + [vmem] * 4,
        out_specs=(vmem,) * 7,
        compiler_params=pltpu.CompilerParams(vmem_limit_bytes=24 << 20),
        interpret=INTERPRET,
        name="pre",
    )(lam, video, fore, mult, dual)


def solve(shrink0, shrink1, packed):
    n = packed.shape[1]
    half = n // 2
    quarter = half // 2
    top = packed[:quarter]
    p = jnp.concatenate([top, pltpu.roll(top, half, 1)], 0)
    i, j = iota((half, n), 0), iota((half, n), 1)
    t = jnp.concatenate([p[:, :half].T] * 2, 1)
    p2 = pltpu.roll(p, half, 1)
    left = j < half
    jj = jnp.where(left, j, j - half)
    p = jnp.where(left, p, p2)
    diag = packed[quarter : quarter + 1]
    diag = jnp.where(left[:1], diag, pltpu.roll(diag, half, 1))
    on = i == jj
    g = jnp.where(left == (i <= jj), p, t)
    g = jnp.where(on & ~left, diag, g)
    dg = jnp.sum(jnp.where(on, g, 0.0), 0, keepdims=True)
    l1 = left[:1]
    tr0 = jnp.sum(jnp.where(l1, dg, 0.0), 1, keepdims=True)
    tr1 = jnp.sum(jnp.where(l1, 0.0, dg), 1, keepdims=True)
    tau = jnp.where(l1, shrink0 * tr0, shrink1 * tr1) * (1.0 / half)
    a = g + jnp.where(on, tau, 0.0)

    pick = jnp.where(left, 0, half)
    for k in range(half):
        col = jnp.take_along_axis(a, pick + k, axis=1)
        d = col[k : k + 1]
        r = 1.0 / d
        at = jj[:1] == k
        s = jnp.where(at, -r, a[k : k + 1] * r)
        col = jnp.where(i == k, -1.0, col)
        a = jnp.where((i == k) | (jj == k), 0.0, a) - col * s
    f = tau * a + jnp.where(on, 1.0, 0.0)
    low = jnp.where(left, f, 0.0)
    return jnp.concatenate([low, f - low], 0)


def tv_kernel(
    where_ref, shrink_ref, lam_ref, packed, data, base, dual,
    row_lo, row_hi, col_lo, col_hi, cor_lo, cor_hi,
    low_out, fore_out, mult_out, dual_out,
    t_ref, qf, qh, qw, low, fore, mult, sem,
):
    tw, th, n = data.shape
    half = n // 2
    eh, ew = th + 2 * M, tw + 2 * M
    row_at, rows, col_at, cols = where_ref[0], where_ref[1], where_ref[2], where_ref[3]
    lane = iota((1, n), 1)
    lam = jnp.where(lane < half, lam_ref[0], lam_ref[1])
    scale = KAPPA / lam
    mask_f = jnp.where((lane == half - 1) | (lane == n - 1), 0.0, 1.0)
    ring = iota((eh, n), 0)
    no_h = ((ring == th - 1) & (row_at == rows - 1)) | ((ring == eh - 1) & (row_at == 0))
    bound_h = jnp.where(no_h, 0.0, 1.0)

    filt = solve(shrink_ref[0], shrink_ref[1], packed[...])
    fh, fl = split(filt)
    weights = jnp.concatenate([jnp.concatenate([fh, fl], 1), jnp.concatenate([fh, jnp.zeros_like(fl)], 1)], 0)

    def low_rank(x):
        hi, lo = split(x)
        y = jnp.dot(jnp.concatenate([hi, lo], 1), weights, preferred_element_type=jnp.float32)
        return y[:, :n] + y[:, n:]

    wide = 4

    def fill(i, _):
        at = pl.ds(i * wide, wide)
        to = pl.ds(i * wide + M, wide)
        y = low_rank(data[at].reshape(wide * th, n)).reshape(wide, th, n)
        low[at] = y
        t_ref[to, :th] = (base[at] - y) * scale
        x = jnp.concatenate([row_hi[0, at], row_lo[0, at]], 1)
        y = low_rank(x.reshape(wide * 2 * M, n)).reshape(wide, 2 * M, n)
        b = jnp.concatenate([row_hi[1, at], row_lo[1, at]], 1)
        t_ref[to, th:] = (b - y) * scale
        for k, q in enumerate((qf, qh, qw)):
            v = dual[k, at]
            e = jnp.concatenate([row_hi[2 + k, at], row_lo[2 + k, at]], 1)
            if k == 0:
                v, e = v * mask_f, e * mask_f
            if k == 1:
                v, e = v * bound_h[:th], e * bound_h[th:]
            q[to, :th] = v
            q[to, th:] = e
        return 0

    lax.fori_loop(0, tw // wide, fill, 0)
    for side, cor, at in ((col_lo, cor_lo, 0), (col_hi, cor_hi, tw + M)):
        to = pl.ds(at, M)
        y = low_rank(side[0].reshape(M * th, n)).reshape(M, th, n)
        t_ref[to, :th] = (side[1] - y) * scale
        x = jnp.concatenate([cor[0, 0], cor[1, 0]], 1)
        y = low_rank(x.reshape(M * 2 * M, n)).reshape(M, 2 * M, n)
        b = jnp.concatenate([cor[0, 1], cor[1, 1]], 1)
        t_ref[to, th:] = (b - y) * scale
        for k, q in enumerate((qf, qh, qw)):
            v = side[2 + k]
            e = jnp.concatenate([cor[0, 2 + k], cor[1, 2 + k]], 1)
            if k == 0:
                v, e = v * mask_f, e * mask_f
            if k == 1:
                v, e = v * bound_h[:th], e * bound_h[th:]
            q[to, :th] = v
            q[to, th:] = e

    def bound_w(e):
        no = ((e == M - 1) & (col_at == 0)) | ((e == tw + M - 1) & (col_at == cols - 1))
        return jnp.where(no, 0.0, 1.0)

    qw[M - 1] = qw[M - 1] * bound_w(M - 1)
    qw[tw + M - 1] = qw[tw + M - 1] * bound_w(tw + M - 1)

    def div(f, h, w, w_prev, first):
        h_prev = pltpu.roll(h, 1, 0)
        if first:
            h_prev = jnp.where(ring == th + M, 0.0, h_prev)
        return (f - pltpu.roll(f, 1, 1)) + (h - h_prev) + (w - w_prev)

    def clip(x, b):
        return jnp.minimum(jnp.maximum(x, -b), b)

    group = tw // sem.shape[0]

    def copies(g):
        at, ext = pl.ds(g * group, group), pl.ds(g * group + M, group)
        pairs = [(low.at[at], low_out.at[at]), (fore.at[at], fore_out.at[at]), (mult.at[at], mult_out.at[at])]
        pairs += [(q.at[ext, pl.ds(0, th)], dual_out.at[k, at]) for k, q in enumerate((qf, qh, qw))]
        return [pltpu.make_async_copy(src, dst, sem.at[g, i]) for i, (src, dst) in enumerate(pairs)]

    inverse = lam * (1.0 / KAPPA)
    for s in range(TV_STEPS):
        first, last = s == 0, s == TV_STEPS - 1

        def field(e, f, h, w, w_prev):
            return t_ref[e] - KAPPA * div(f, h, w, w_prev, first)

        def body(e, carry):
            f, h, w, v, w_done = carry
            f1, h1, w1 = qf[e + 1], qh[e + 1], qw[e + 1]
            v1 = field(e + 1, f1, h1, w1, w)
            f = clip(f + (pltpu.roll(v, n - 1, 1) - v), mask_f)
            h = clip(h + (pltpu.roll(v, eh - 1, 0) - v), bound_h)
            w = clip(w + (v1 - v), bound_w(e))
            if last:
                c = e - M
                h_prev = pltpu.roll(h, 1, 0)[:th]
                lift = (f[:th] - pltpu.roll(f[:th], 1, 1)) + (h[:th] - h_prev) + (w[:th] - w_done)
                lift = lift * lam
                fore[c] = t_ref[e, :th] * inverse - lift
                mult[c] = lift * MU
                qf[e, :th] = jnp.where(mask_f > 0.0, f[:th], dual[0, c])
                qh[e, :th] = jnp.where(bound_h[:th] > 0.0, h[:th], dual[1, c])
                qw[e, :th] = w[:th]
                w_done = w[:th]
            else:
                qf[e], qh[e], qw[e] = f, h, w
            return f1, h1, w1, v1, w_done

        f, h, w = qf[s], qh[s], qw[s]
        w_prev = jnp.zeros_like(w) if first else qw[s - 1]
        v = field(s, f, h, w, w_prev)
        carry = (f, h, w, v, jnp.zeros((th, n), jnp.float32))
        if not last:
            lax.fori_loop(s, ew - 1 - s, body, carry)
        else:
            f1, h1, w1 = qf[s + 1], qh[s + 1], qw[s + 1]
            v1 = field(s + 1, f1, h1, w1, w)
            w_done = clip(w + (v1 - v), bound_w(s))[:th]
            carry = (f1, h1, w1, v1, w_done)
            groups = sem.shape[0]
            for g in range(groups):
                carry = lax.fori_loop(M + g * group, M + (g + 1) * group, body, carry)
                if g == groups - 1:

                    @pl.when(col_at == cols - 1)
                    def _():
                        qw[tw + M - 1, :th] = dual[2, tw - 1]

                for copy in copies(g):
                    copy.start()
            for g in range(groups):
                for copy in copies(g):
                    copy.wait()


def tv(where, shrink, lam, packed, data, base, dual, *halos):
    tw, th, n = data.shape
    f32 = lambda *s: jax.ShapeDtypeStruct(s, jnp.float32)
    vmem = pl.BlockSpec(memory_space=pltpu.VMEM)
    smem = pl.BlockSpec(memory_space=pltpu.SMEM)
    big = pltpu.VMEM((tw + 2 * M, th + 2 * M, n), jnp.float32)
    return pl.pallas_call(
        tv_kernel,
        out_shape=(f32(tw, th, n),) * 3 + (f32(3, tw, th, n),),
        in_specs=[smem] * 3 + [vmem] * (4 + len(halos)),
        out_specs=(pl.BlockSpec(memory_space=pl.ANY),) * 4,
        scratch_shapes=[big] * 4 + [pltpu.VMEM((tw, th, n), jnp.float32)] * 3 + [pltpu.SemaphoreType.DMA((GROUPS, 6))],
        compiler_params=pltpu.CompilerParams(vmem_limit_bytes=32 << 20),
        interpret=INTERPRET,
        name="tv",
    )(where, shrink, lam, packed, data, base, dual, *halos)


def local(video, fore_prev, mult, dual_tv, shrink, tv_weight):
    tw = fore_prev.shape[0]
    rows, cols = lax.axis_size("rows"), lax.axis_size("cols")
    up = lambda n: [(i, i + 1) for i in range(n - 1)]
    down = lambda n: [(i + 1, i) for i in range(n - 1)]
    gram, data, base, row_lo, row_hi, col_lo, col_hi = pre(tv_weight, video, fore_prev, mult, dual_tv)
    row_lo = lax.ppermute(row_lo, "rows", up(rows))
    row_hi = lax.ppermute(row_hi, "rows", down(rows))
    col_lo = lax.ppermute(col_lo, "cols", up(cols))
    col_hi = lax.ppermute(col_hi, "cols", down(cols))
    cor_lo = lax.ppermute(jnp.stack([row_hi[:, tw - M :], row_lo[:, tw - M :]]), "cols", up(cols))
    cor_hi = lax.ppermute(jnp.stack([row_hi[:, :M], row_lo[:, :M]]), "cols", down(cols))
    for axis, to in reduction_rounds(rows, cols):
        gram = gram + lax.ppermute(gram, axis, list(enumerate(to)))
    where = jnp.stack([lax.axis_index("rows"), rows, lax.axis_index("cols"), cols]).astype(jnp.int32)
    return tv(where, shrink, tv_weight, gram, data, base, dual_tv, row_lo, row_hi, col_lo, col_hi, cor_lo, cor_hi)


def solution(mesh):
    tile = P("cols", "rows", None)
    duals = P(None, "cols", "rows", None)
    return jax.shard_map(
        local,
        mesh=mesh,
        in_specs=(tile, tile, tile, duals, P(), P()),
        out_specs=(tile, tile, tile, duals),
        check_vma=False,
    )
```

```python
import functools

import jax
import jax.numpy as jnp
from jax import lax
from jax.experimental import pallas as pl
from jax.experimental.pallas import tpu as pltpu
from jax.sharding import PartitionSpec as P


TV_STEPS = 4
MU = 1.25
KAPPA = 0.08
M = 4
CORES = 2
GROUPS = 6
NY = 4
INTERPRET = False
UNROLL = 6
WAIT_AT = 24
TV_LIMIT = 53
CORNER_LIMIT = 40
UNROLL_LAST = 5


def ring_rounds(n):
    if n == 1:
        return []
    if n == 2:
        return [[1, 0]]
    even = [i ^ 1 for i in range(n)]
    odd = [(i + 1) % n if i % 2 else (i - 1) % n for i in range(n)]
    if n == 4:
        return [even, odd]
    assert n == 8
    return [even, odd, [3, 6, 5, 0, 7, 2, 1, 4]]


def reduction_rounds(rows, cols):
    nx, nz = rows // CORES, cols // NY
    out = [("rows", [r ^ 1 for r in range(rows)])]
    for to in ring_rounds(NY):
        out.append(("cols", [c // NY * NY + to[c % NY] for c in range(cols)]))
    for to in ring_rounds(nz):
        out.append(("cols", [to[c // NY] * NY + c % NY for c in range(cols)]))
    for to in ring_rounds(nx):
        out.append(("rows", [to[r // CORES] * CORES + r % CORES for r in range(rows)]))
    return out


def iota(shape, dim):
    return lax.broadcasted_iota(jnp.int32, shape, dim)


def split(x):
    hi = x.astype(jnp.bfloat16)
    return hi, (x - hi.astype(jnp.float32)).astype(jnp.bfloat16)


VMEM = pl.BlockSpec(memory_space=pltpu.VMEM)
SMEM = pl.BlockSpec(memory_space=pltpu.SMEM)
ANY = pl.BlockSpec(memory_space=pl.ANY)


def f32(*shape):
    return jax.ShapeDtypeStruct(shape, jnp.float32)


def call(kernel, outs, limit, ins, out_specs=None, scratch=(), flops=0):
    return pl.pallas_call(
        kernel,
        out_shape=outs,
        in_specs=ins,
        out_specs=out_specs or (VMEM,) * len(outs),
        scratch_shapes=scratch,
        compiler_params=pltpu.CompilerParams(vmem_limit_bytes=int(limit * 2**20)),
        cost_estimate=pl.CostEstimate(flops=flops, bytes_accessed=1 << 20, transcendentals=0),
        interpret=INTERPRET,
    )


def gram_kernel(video_hbm, fore_hbm, mult_hbm, gram, video, fore, mult, sem):
    tw, th, n = fore.shape
    half, quarter = n // 2, n // 4
    parts = sem.shape[0]
    step = tw // parts

    def copies(g):
        at = pl.ds(g * step, step)
        pairs = [(video_hbm, video), (fore_hbm, fore), (mult_hbm, mult)]
        return [pltpu.make_async_copy(src.at[at], dst.at[at], sem.at[g, i]) for i, (src, dst) in enumerate(pairs)]

    for g in range(parts):
        for copy in copies(g):
            copy.start()
    acc = jnp.zeros((n, 2 * n), jnp.float32)
    for g in range(parts):
        for copy in copies(g):
            copy.wait()
        at = pl.ds(g * step, step)
        b = video[at].astype(jnp.float32) + mult[at] * (1.0 / MU)
        d = b - fore[at]
        hi, lo = split(d.reshape(step * th, n))
        acc += lax.dot_general(
            hi, jnp.concatenate([hi, lo], 1), (((0,), (0,)), ((), ())), preferred_element_type=jnp.float32
        )
    i, j = iota((half, n), 0), iota((half, n), 1)
    cross = jnp.where(j < half, acc[:half, n:], acc[half:, n:])
    whole = jnp.where(j < half, acc[:half, :n], acc[half:, :n]) + cross
    whole = whole + jnp.concatenate([cross[:, :half].T, cross[:, half:].T], 1)
    other = pltpu.roll(whole, half, 1)
    packed = jnp.where(i <= j, whole, other)
    diag = jnp.sum(jnp.where(i == j, other, 0.0), 0, keepdims=True)
    gram[:quarter] = jnp.where(j[:quarter] < half, packed[:quarter], pltpu.roll(packed[quarter:], half, 1))
    gram[quarter:] = jnp.broadcast_to(diag, (8, n))


def make_gram(video, fore, mult):
    tw, th, n = fore.shape
    full = pltpu.VMEM((tw, th, n), jnp.float32)
    return call(
        gram_kernel,
        (f32(n // 4 + 8, n),),
        53.8,
        [ANY] * 3,
        scratch=[pltpu.VMEM((tw, th, n), video.dtype), full, full, pltpu.SemaphoreType.DMA((5, 3))],
        flops=1 << 28,
    )(video, fore, mult)[0]


def lane_of(n, ref):
    return jnp.where(iota((1, n), 1) < n // 2, ref[0], ref[1])


def pack_kernel(by_row, lam_ref, video_hbm, fore_hbm, mult_hbm, dual_hbm, lo_out, hi_out, lo, hi, video, fore, mult, dual, in_sem, out_sem):
    tw, th, n = fore_hbm.shape
    ends = (pl.ds(0, 8), pl.ds((th if by_row else tw) - 8, 8))

    def strip(ref, side):
        return ref.at[:, ends[side]] if by_row else ref.at[ends[side]]

    arrive = []
    for side in range(2):
        pairs = [(video_hbm, video.at[side]), (fore_hbm, fore.at[side]), (mult_hbm, mult.at[side])]
        pairs += [(dual_hbm.at[k], dual.at[side, k]) for k in range(3)]
        arrive.append([pltpu.make_async_copy(strip(x, side), y, in_sem.at[side, i]) for i, (x, y) in enumerate(pairs)])
    for copies in arrive:
        for copy in copies:
            copy.start()
    lam = lane_of(n, lam_ref)
    leave = []

    def send(side, k):
        src, dst = ((hi, hi_out), (lo, lo_out))[side]
        copy = pltpu.make_async_copy(src.at[k], dst.at[k], out_sem.at[side, k])
        copy.start()
        leave.append(copy)

    def part(x, side):
        at = slice(8 - M, None) if side else slice(None, M)
        return x[:, at] if by_row else x[at]

    for side, out in enumerate((hi, lo)):
        for copy in arrive[side]:
            copy.wait()
        for k in range(3):
            out[2 + k] = part(dual[side, k], side)
            send(side, 2 + k)
        b = video[side].astype(jnp.float32) + mult[side] * (1.0 / MU)
        out[0] = part(b - fore[side], side)
        send(side, 0)
        out[1] = part(b, side)
        if side and by_row:
            out[1, :, 0:1, :] = b[:, 8 - M : 9 - M] + lam[None] * dual[side, 1, :, 7 - M : 8 - M]
        elif side:
            out[1, 0] = b[8 - M] + lam * dual[side, 2, 7 - M]
        send(side, 1)
    for copy in leave:
        copy.wait()


def pack(by_row, lam, video, fore, mult, dual):
    tw, th, n = fore.shape
    out = (5, tw, M, n) if by_row else (5, M, th, n)
    strip = (tw, 8, n) if by_row else (8, th, n)
    return call(
        functools.partial(pack_kernel, by_row),
        (f32(*out),) * 2,
        63,
        [SMEM] + [ANY] * 4,
        (ANY,) * 2,
        [pltpu.VMEM(out, jnp.float32)] * 2
        + [pltpu.VMEM((2,) + strip, video.dtype)]
        + [pltpu.VMEM((2,) + strip, jnp.float32)] * 2
        + [pltpu.VMEM((2, 3) + strip, jnp.float32), pltpu.SemaphoreType.DMA((2, 6)), pltpu.SemaphoreType.DMA((2, 5))],
        flops=1 << 20,
    )(lam, video, fore, mult, dual)


def corner_kernel(row_lo, row_hi, cor_lo, cor_hi, sem):
    tw = row_lo.shape[1]
    copies = []
    for k, x in enumerate((row_hi, row_lo)):
        copies += [(x.at[:, pl.ds(0, M)], cor_hi.at[k]), (x.at[:, pl.ds(tw - M, M)], cor_lo.at[k])]
    copies = [pltpu.make_async_copy(src, dst, sem.at[i]) for i, (src, dst) in enumerate(copies)]
    for copy in copies:
        copy.start()
    for copy in copies:
        copy.wait()


def corners(row_lo, row_hi):
    n = row_lo.shape[-1]
    outs = (f32(2, 5, M, M, n),) * 2
    return call(
        corner_kernel, outs, CORNER_LIMIT, [ANY] * 2, scratch=[pltpu.SemaphoreType.DMA((4,))], flops=1 << 20
    )(row_lo, row_hi)


def masks(where_ref, th, n):
    row_at, rows = where_ref[0], where_ref[1]
    lane = iota((1, n), 1)
    mask_f = jnp.where((lane == n // 2 - 1) | (lane == n - 1), 0.0, 1.0)
    ring = iota((th + 2 * M, n), 0)
    none = ((ring == th - 1) & (row_at == rows - 1)) | ((ring == th + 2 * M - 1) & (row_at == 0))
    return mask_f, jnp.where(none, 0.0, 1.0), ring


def bound_w(where_ref, e, tw):
    col_at, cols = where_ref[2], where_ref[3]
    none = ((e == M - 1) & (col_at == 0)) | ((e == tw + M - 1) & (col_at == cols - 1))
    return jnp.where(none, 0.0, 1.0)


def solve(shrink0, shrink1, packed, between):
    n = packed.shape[1]
    half = n // 2
    quarter = half // 2
    top = packed[:quarter]
    p = jnp.concatenate([top, pltpu.roll(top, half, 1)], 0)
    i, j = iota((half, n), 0), iota((half, n), 1)
    t = jnp.concatenate([p[:, :half].T] * 2, 1)
    left = j < half
    jj = jnp.where(left, j, j - half)
    p = jnp.where(left, p, pltpu.roll(p, half, 1))
    diag = packed[quarter : quarter + 1]
    diag = jnp.where(left[:1], diag, pltpu.roll(diag, half, 1))
    on = i == jj
    g = jnp.where(left == (i <= jj), p, t)
    g = jnp.where(on & ~left, diag, g)
    dg = jnp.sum(jnp.where(on, g, 0.0), 0, keepdims=True)
    l1 = left[:1]
    tr0 = jnp.sum(jnp.where(l1, dg, 0.0), 1, keepdims=True)
    tr1 = jnp.sum(jnp.where(l1, 0.0, dg), 1, keepdims=True)
    tau = jnp.where(l1, shrink0 * tr0, shrink1 * tr1) * (1.0 / half)
    a = g + jnp.where(on, tau, 0.0)

    pick = jnp.where(left, 0, half)
    for k in range(half):
        col = jnp.take_along_axis(a, pick + k, axis=1)
        d = col[k : k + 1]
        r = 1.0 / d
        at = jj[:1] == k
        s = jnp.where(at, -r, a[k : k + 1] * r)
        col = jnp.where(i == k, -1.0, col)
        a = jnp.where((i == k) | (jj == k), 0.0, a) - col * s
        between(k, half)
    f = tau * a + jnp.where(on, 1.0, 0.0)
    low = jnp.where(left, f, 0.0)
    return jnp.concatenate([low, f - low], 0)


def tv_kernel(
    where_ref, shrink_ref, lam_ref, packed,
    video_in, fore_in, mult_in, dual_in, row_lo_in, row_hi_in, col_lo_in, col_hi_in, cor_lo_in, cor_hi_in,
    low_out, fore_out, mult_out, dual_out,
    video, fore, mult, dual, row_lo, row_hi, col_lo, col_hi, cor_lo, cor_hi,
    x2, t_ref, qf, qh, qw, low, in_sem, sem, low_sem,
):
    tw, th, n = low.shape
    eh, ew = th + 2 * M, tw + 2 * M
    arrive = [
        pltpu.make_async_copy(src, dst, in_sem.at[i])
        for i, (src, dst) in enumerate(
            zip(
                (video_in, fore_in, mult_in, dual_in, row_lo_in, row_hi_in, col_lo_in, col_hi_in, cor_lo_in, cor_hi_in),
                (video, fore, mult, dual, row_lo, row_hi, col_lo, col_hi, cor_lo, cor_hi),
                strict=True,
            )
        )
    ]
    for copy in arrive:
        copy.start()
    lam = lane_of(n, lam_ref)
    scale = KAPPA / lam
    mask_f, bound_h, ring = masks(where_ref, th, n)

    def put(e):
        if M <= e < tw + M:
            at = pl.ds(e - M, 2)
            b = video[at].astype(jnp.float32) + mult[at] * (1.0 / MU)
            tile = [b - fore[at], b, dual[0, at], dual[1, at], dual[2, at]]
            tile = [jnp.concatenate([x, row_hi[k, at], row_lo[k, at]], 1) for k, x in enumerate(tile)]
        else:
            side, cor = (col_lo, cor_lo) if e < M else (col_hi, cor_hi)
            at = pl.ds(e if e < M else e - tw - M, 2)
            tile = [jnp.concatenate([side[k, at], cor[0, k, at], cor[1, k, at]], 1) for k in range(5)]
        hi, lo = split(tile[0].reshape(2 * eh, n))
        x2[e * eh : (e + 2) * eh] = jnp.concatenate([hi, lo], 1)
        at = pl.ds(e, 2)
        t_ref[at] = tile[1]
        qf[at] = tile[2] * mask_f
        qh[at] = tile[3] * bound_h
        qw[at] = tile[4]
        for x in (M - 1, tw + M - 1):
            if x in (e, e + 1):
                qw[x] = tile[4][x - e] * bound_w(where_ref, x, tw)

    def between(k, steps):
        if k == WAIT_AT:
            for copy in arrive:
                copy.wait()
        if k >= WAIT_AT:
            span, units = steps - WAIT_AT, ew // 2
            for u in range((k - WAIT_AT) * units // span, (k + 1 - WAIT_AT) * units // span):
                put(2 * u)

    filt = solve(shrink_ref[0], shrink_ref[1], packed[...], between)
    fh, fl = split(filt)
    weights = jnp.concatenate([jnp.concatenate([fh, fl], 1), jnp.concatenate([fh, jnp.zeros_like(fl)], 1)], 0)

    def low_copy(g, part):
        at = pl.ds(g * part, part)
        return pltpu.make_async_copy(low.at[at], low_out.at[at], low_sem.at[g])

    def low_rank(e, size):
        y = jnp.dot(x2[e * eh : (e + size) * eh], weights, preferred_element_type=jnp.float32)
        y = (y[:, :n] + y[:, n:]).reshape(size, eh, n)
        t_ref[e : e + size] = (t_ref[e : e + size] - y) * scale
        return y

    part = tw // low_sem.shape[0]
    low_rank(0, M)
    for g in range(low_sem.shape[0]):
        low[g * part : (g + 1) * part] = low_rank(M + g * part, part)[:, :th]
        low_copy(g, part).start()
    low_rank(tw + M, M)

    def clip(x, b):
        return jnp.minimum(jnp.maximum(x, -b), b)

    groups = sem.shape[0]
    group = tw // groups

    def copies(g):
        at, ext = pl.ds(g * group, group), pl.ds(g * group + M, group)
        pairs = [(fore.at[at], fore_out.at[at]), (mult.at[at], mult_out.at[at])]
        pairs += [(q.at[ext, pl.ds(0, th)], dual_out.at[k, at]) for k, q in enumerate((qf, qh, qw))]
        return [pltpu.make_async_copy(src, dst, sem.at[g, i]) for i, (src, dst) in enumerate(pairs)]

    inverse = lam * (1.0 / KAPPA)
    for s in range(TV_STEPS):
        first, last = s == 0, s == TV_STEPS - 1

        def field(e, f, h, w, w_prev):
            h_prev = pltpu.roll(h, 1, 0)
            if first:
                h_prev = jnp.where(ring == th + M, 0.0, h_prev)
            return t_ref[e] - KAPPA * ((f - pltpu.roll(f, 1, 1)) + (h - h_prev) + (w - w_prev))

        def body(e, carry):
            f, h, w, v, w_done = carry
            f1, h1, w1 = qf[e + 1], qh[e + 1], qw[e + 1]
            v1 = field(e + 1, f1, h1, w1, w)
            f = clip(f + (pltpu.roll(v, n - 1, 1) - v), mask_f)
            h = clip(h + (pltpu.roll(v, eh - 1, 0) - v), bound_h)
            w = clip(w + (v1 - v), bound_w(where_ref, e, tw))
            if last:
                c = e - M
                f, h_prev, h, w = f[:th], pltpu.roll(h, 1, 0)[:th], h[:th], w[:th]
                lift = ((f - pltpu.roll(f, 1, 1)) + (h - h_prev) + (w - w_done)) * lam
                fore[c] = t_ref[e, :th] * inverse - lift
                mult[c] = lift * MU
                qf[e, :th] = jnp.where(mask_f > 0.0, f, dual[0, c])
                qh[e, :th] = jnp.where(bound_h[:th] > 0.0, h, dual[1, c])
                qw[e, :th] = w
                w_done = w
            else:
                qf[e], qh[e], qw[e] = f, h, w
            return f1, h1, w1, v1, w_done

        f, h, w = qf[s], qh[s], qw[s]
        v = field(s, f, h, w, jnp.zeros_like(w) if first else qw[s - 1])
        carry = (f, h, w, v, jnp.zeros((th, n), jnp.float32))
        if not last:
            lax.fori_loop(s, ew - 1 - s, body, carry, unroll=UNROLL)
        else:
            f1, h1, w1 = qf[s + 1], qh[s + 1], qw[s + 1]
            v1 = field(s + 1, f1, h1, w1, w)
            w_done = clip(w + (v1 - v), bound_w(where_ref, s, tw))[:th]
            carry = (f1, h1, w1, v1, w_done)
            for g in range(groups):
                carry = lax.fori_loop(M + g * group, M + (g + 1) * group, body, carry, unroll=UNROLL_LAST)
                if g == groups - 1:

                    @pl.when(where_ref[2] == where_ref[3] - 1)
                    def _():
                        qw[tw + M - 1, :th] = dual[2, tw - 1]

                for copy in copies(g):
                    copy.start()
    for g in range(low_sem.shape[0]):
        low_copy(g, part).wait()
    for g in range(groups):
        for copy in copies(g):
            copy.wait()


def tv(where, shrink, lam, packed, video, *arrays):
    tw, th, n = video.shape
    ew, eh = tw + 2 * M, th + 2 * M
    inputs = [pltpu.VMEM(x.shape, x.dtype) for x in (video,) + arrays]
    return call(
        tv_kernel,
        (f32(tw, th, n),) * 3 + (f32(3, tw, th, n),),
        TV_LIMIT,
        [SMEM] * 3 + [VMEM] + [ANY] * len(inputs),
        (ANY,) * 4,
        inputs
        + [pltpu.VMEM((ew * eh, 2 * n), jnp.bfloat16)]
        + [pltpu.VMEM((ew, eh, n), jnp.float32)] * 4
        + [pltpu.VMEM((tw, th, n), jnp.float32)]
        + [pltpu.SemaphoreType.DMA((len(inputs),)), pltpu.SemaphoreType.DMA((GROUPS, 5)), pltpu.SemaphoreType.DMA((3,))],
        flops=1 << 30,
    )(where, shrink, lam, packed, video, *arrays)


def local(video, fore_prev, mult, dual_tv, shrink, tv_weight):
    rows, cols = lax.axis_size("rows"), lax.axis_size("cols")
    up = lambda n: [(i, i + 1) for i in range(n - 1)]
    down = lambda n: [(i + 1, i) for i in range(n - 1)]
    where = jnp.stack([lax.axis_index("rows"), rows, lax.axis_index("cols"), cols]).astype(jnp.int32)
    gram = make_gram(video, fore_prev, mult)
    row_lo, row_hi = pack(True, tv_weight, video, fore_prev, mult, dual_tv)
    col_lo, col_hi = pack(False, tv_weight, video, fore_prev, mult, dual_tv)
    row_lo = lax.ppermute(row_lo, "rows", up(rows))
    row_hi = lax.ppermute(row_hi, "rows", down(rows))
    col_lo = lax.ppermute(col_lo, "cols", up(cols))
    col_hi = lax.ppermute(col_hi, "cols", down(cols))
    cor_lo, cor_hi = corners(row_lo, row_hi)
    cor_lo = lax.ppermute(cor_lo, "cols", up(cols))
    cor_hi = lax.ppermute(cor_hi, "cols", down(cols))
    for axis, to in reduction_rounds(rows, cols):
        gram = gram + lax.ppermute(gram, axis, list(enumerate(to)))
    halos = (row_lo, row_hi, col_lo, col_hi, cor_lo, cor_hi)
    return tv(where, shrink, tv_weight, gram, video, fore_prev, mult, dual_tv, *halos)


def solution(mesh):
    tile = P("cols", "rows", None)
    duals = P(None, "cols", "rows", None)
    return jax.shard_map(
        local,
        mesh=mesh,
        in_specs=(tile, tile, tile, duals, P(), P()),
        out_specs=(tile, tile, tile, duals),
        check_vma=False,
    )
```

```python
import jax
import jax.numpy as jnp
from jax import lax
from jax.experimental import pallas as pl
from jax.experimental.pallas import tpu as pltpu
from jax.sharding import PartitionSpec as P


TV_STEPS = 4
MU = 1.25
KAPPA = 0.08
M = 4
CORES = 2
GROUPS = 6
NY = 4
INTERPRET = False
UNROLL = 11
WAIT_AT = 24
TV_LIMIT = 53
GRAM_LIMIT = 63
CORNER_LIMIT = 40
UNROLL_LAST = 10


def ring_rounds(n):
    if n == 1:
        return []
    if n == 2:
        return [[1, 0]]
    even = [i ^ 1 for i in range(n)]
    odd = [(i + 1) % n if i % 2 else (i - 1) % n for i in range(n)]
    if n == 4:
        return [even, odd]
    assert n == 8
    return [even, odd, [3, 6, 5, 0, 7, 2, 1, 4]]


def reduction_rounds(rows, cols):
    nx, nz = rows // CORES, cols // NY
    out = [("rows", [r ^ 1 for r in range(rows)])]
    for to in ring_rounds(NY):
        out.append(("cols", [c // NY * NY + to[c % NY] for c in range(cols)]))
    for to in ring_rounds(nz):
        out.append(("cols", [to[c // NY] * NY + c % NY for c in range(cols)]))
    for to in ring_rounds(nx):
        out.append(("rows", [to[r // CORES] * CORES + r % CORES for r in range(rows)]))
    return out


def iota(shape, dim):
    return lax.broadcasted_iota(jnp.int32, shape, dim)


def split(x):
    hi = x.astype(jnp.bfloat16)
    return hi, (x - hi.astype(jnp.float32)).astype(jnp.bfloat16)


VMEM = pl.BlockSpec(memory_space=pltpu.VMEM)
SMEM = pl.BlockSpec(memory_space=pltpu.SMEM)
ANY = pl.BlockSpec(memory_space=pl.ANY)


def f32(*shape):
    return jax.ShapeDtypeStruct(shape, jnp.float32)


def call(kernel, outs, limit, ins, out_specs=None, scratch=(), flops=0):
    return pl.pallas_call(
        kernel,
        out_shape=outs,
        in_specs=ins,
        out_specs=out_specs or (VMEM,) * len(outs),
        scratch_shapes=scratch,
        compiler_params=pltpu.CompilerParams(vmem_limit_bytes=int(limit * 2**20)),
        cost_estimate=pl.CostEstimate(flops=flops, bytes_accessed=1 << 20, transcendentals=0),
        interpret=INTERPRET,
    )


def lane_of(n, ref):
    return jnp.where(iota((1, n), 1) < n // 2, ref[0], ref[1])


def gram_kernel(
    lam_ref, video_hbm, fore_hbm, mult_hbm, dual_hbm,
    gram, row_lo_out, row_hi_out, col_lo_out, col_hi_out,
    row_lo, row_hi, col_lo, col_hi, video, fore, mult, by_row, by_col, sem, strip_sem, out_sem,
):
    tw, th, n = fore.shape
    half, quarter = n // 2, n // 4
    parts = sem.shape[0]
    step = tw // parts

    def copies(g):
        at = pl.ds(g * step, step)
        pairs = [(video_hbm, video), (fore_hbm, fore), (mult_hbm, mult)]
        return [pltpu.make_async_copy(src.at[at], dst.at[at], sem.at[g, i]) for i, (src, dst) in enumerate(pairs)]

    strips = []
    for side in range(2):
        pairs = [(dual_hbm.at[:, :, pl.ds((0, th - 8)[side], 8)], by_row.at[side])]
        pairs += [(dual_hbm.at[:, pl.ds((0, tw - 8)[side], 8)], by_col.at[side])]
        strips += [pltpu.make_async_copy(x, y, strip_sem.at[side, i]) for i, (x, y) in enumerate(pairs)]
    for g in range(parts):
        for copy in copies(g):
            copy.start()
    for copy in strips:
        copy.start()
    leave = []

    def send(k):
        pairs = [(row_lo, row_lo_out), (row_hi, row_hi_out), (col_lo, col_lo_out), (col_hi, col_hi_out)]
        new = [pltpu.make_async_copy(x.at[k], y.at[k], out_sem.at[i, k]) for i, (x, y) in enumerate(pairs)]
        for copy in new:
            copy.start()
        leave.extend(new)

    acc = jnp.zeros((n, 2 * n), jnp.float32)
    for g in range(parts):
        for copy in copies(g):
            copy.wait()
        at = pl.ds(g * step, step)
        b = video[at].astype(jnp.float32) + mult[at] * (1.0 / MU)
        d = b - fore[at]
        for k, x in enumerate((d, b)):
            row_hi[k, at] = x[:, :M]
            row_lo[k, at] = x[:, th - M :]
            if g == 0:
                col_hi[k] = x[:M]
            if g == parts - 1:
                col_lo[k] = x[step - M :]
        hi, lo = split(d.reshape(step * th, n))
        acc += lax.dot_general(
            hi, jnp.concatenate([hi, lo], 1), (((0,), (0,)), ((), ())), preferred_element_type=jnp.float32
        )
    send(0)
    for copy in strips:
        copy.wait()
    for k in range(3):
        row_hi[2 + k] = by_row[0, k, :, :M]
        row_lo[2 + k] = by_row[1, k, :, 8 - M :]
        col_hi[2 + k] = by_col[0, k, :M]
        col_lo[2 + k] = by_col[1, k, 8 - M :]
        send(2 + k)
    lam = lane_of(n, lam_ref)
    row_lo[1, :, 0:1, :] = row_lo[1, :, 0:1, :] + lam[None] * by_row[1, 1, :, 7 - M : 8 - M]
    col_lo[1, 0] = col_lo[1, 0] + lam * by_col[1, 2, 7 - M]
    send(1)
    i, j = iota((half, n), 0), iota((half, n), 1)
    cross = jnp.where(j < half, acc[:half, n:], acc[half:, n:])
    whole = jnp.where(j < half, acc[:half, :n], acc[half:, :n]) + cross
    whole = whole + jnp.concatenate([cross[:, :half].T, cross[:, half:].T], 1)
    other = pltpu.roll(whole, half, 1)
    packed = jnp.where(i <= j, whole, other)
    diag = jnp.sum(jnp.where(i == j, other, 0.0), 0, keepdims=True)
    gram[:quarter] = jnp.where(j[:quarter] < half, packed[:quarter], pltpu.roll(packed[quarter:], half, 1))
    gram[quarter:] = jnp.broadcast_to(diag, (8, n))
    for copy in leave:
        copy.wait()


def make_gram(lam, video, fore, mult, dual):
    tw, th, n = fore.shape
    full = pltpu.VMEM((tw, th, n), jnp.float32)
    halos = ((5, tw, M, n),) * 2 + ((5, M, th, n),) * 2
    return call(
        gram_kernel,
        (f32(n // 4 + 8, n),) + tuple(f32(*x) for x in halos),
        GRAM_LIMIT,
        [SMEM] + [ANY] * 4,
        (VMEM,) + (ANY,) * 4,
        [pltpu.VMEM(x, jnp.float32) for x in halos]
        + [pltpu.VMEM((tw, th, n), video.dtype), full, full]
        + [pltpu.VMEM((2, 3, tw, 8, n), jnp.float32), pltpu.VMEM((2, 3, 8, th, n), jnp.float32)]
        + [pltpu.SemaphoreType.DMA((5, 3)), pltpu.SemaphoreType.DMA((2, 2)), pltpu.SemaphoreType.DMA((4, 5))],
        flops=1 << 28,
    )(lam, video, fore, mult, dual)


def corner_kernel(row_lo, row_hi, cor_lo, cor_hi, sem):
    tw = row_lo.shape[1]
    copies = []
    for k, x in enumerate((row_hi, row_lo)):
        copies += [(x.at[:, pl.ds(0, M)], cor_hi.at[k]), (x.at[:, pl.ds(tw - M, M)], cor_lo.at[k])]
    copies = [pltpu.make_async_copy(src, dst, sem.at[i]) for i, (src, dst) in enumerate(copies)]
    for copy in copies:
        copy.start()
    for copy in copies:
        copy.wait()


def corners(row_lo, row_hi):
    n = row_lo.shape[-1]
    outs = (f32(2, 5, M, M, n),) * 2
    return call(
        corner_kernel, outs, CORNER_LIMIT, [ANY] * 2, scratch=[pltpu.SemaphoreType.DMA((4,))], flops=1 << 20
    )(row_lo, row_hi)


def masks(where_ref, th, n):
    row_at, rows = where_ref[0], where_ref[1]
    lane = iota((1, n), 1)
    mask_f = jnp.where((lane == n // 2 - 1) | (lane == n - 1), 0.0, 1.0)
    ring = iota((th + 2 * M, n), 0)
    none = ((ring == th - 1) & (row_at == rows - 1)) | ((ring == th + 2 * M - 1) & (row_at == 0))
    return mask_f, jnp.where(none, 0.0, 1.0), ring


def bound_w(where_ref, e, tw):
    col_at, cols = where_ref[2], where_ref[3]
    none = ((e == M - 1) & (col_at == 0)) | ((e == tw + M - 1) & (col_at == cols - 1))
    return jnp.where(none, 0.0, 1.0)


def solve(shrink0, shrink1, packed, between):
    n = packed.shape[1]
    half = n // 2
    quarter = half // 2
    top = packed[:quarter]
    p = jnp.concatenate([top, pltpu.roll(top, half, 1)], 0)
    i, j = iota((half, n), 0), iota((half, n), 1)
    t = jnp.concatenate([p[:, :half].T] * 2, 1)
    left = j < half
    jj = jnp.where(left, j, j - half)
    p = jnp.where(left, p, pltpu.roll(p, half, 1))
    diag = packed[quarter : quarter + 1]
    diag = jnp.where(left[:1], diag, pltpu.roll(diag, half, 1))
    on = i == jj
    g = jnp.where(left == (i <= jj), p, t)
    g = jnp.where(on & ~left, diag, g)
    dg = jnp.sum(jnp.where(on, g, 0.0), 0, keepdims=True)
    l1 = left[:1]
    tr0 = jnp.sum(jnp.where(l1, dg, 0.0), 1, keepdims=True)
    tr1 = jnp.sum(jnp.where(l1, 0.0, dg), 1, keepdims=True)
    tau = jnp.where(l1, shrink0 * tr0, shrink1 * tr1) * (1.0 / half)
    a = g + jnp.where(on, tau, 0.0)

    pick = jnp.where(left, 0, half)
    for k in range(half):
        col = jnp.take_along_axis(a, pick + k, axis=1)
        d = col[k : k + 1]
        r = 1.0 / d
        at = jj[:1] == k
        s = jnp.where(at, -r, a[k : k + 1] * r)
        col = jnp.where(i == k, -1.0, col)
        a = jnp.where((i == k) | (jj == k), 0.0, a) - col * s
        between(k, half)
    f = tau * a + jnp.where(on, 1.0, 0.0)
    low = jnp.where(left, f, 0.0)
    return jnp.concatenate([low, f - low], 0)


def tv_kernel(
    where_ref, shrink_ref, lam_ref, packed,
    video_in, fore_in, mult_in, dual_in, row_lo_in, row_hi_in, col_lo_in, col_hi_in, cor_lo_in, cor_hi_in,
    low_out, fore_out, mult_out, dual_out,
    video, fore, mult, dual, row_lo, row_hi, col_lo, col_hi, cor_lo, cor_hi,
    x2, t_ref, qf, qh, qw, fore_res, mult_res, low, in_sem, sem, low_sem,
):
    tw, th, n = low.shape
    eh, ew = th + 2 * M, tw + 2 * M
    arrive = [
        pltpu.make_async_copy(src, dst, in_sem.at[i])
        for i, (src, dst) in enumerate(
            zip(
                (video_in, fore_in, mult_in, dual_in, row_lo_in, row_hi_in, col_lo_in, col_hi_in, cor_lo_in, cor_hi_in),
                (video, fore, mult, dual, row_lo, row_hi, col_lo, col_hi, cor_lo, cor_hi),
                strict=True,
            )
        )
    ]
    for copy in arrive:
        copy.start()
    lam = lane_of(n, lam_ref)
    scale = KAPPA / lam
    mask_f, bound_h, _ = masks(where_ref, th, n)

    def put(e):
        if M <= e < tw + M:
            at = pl.ds(e - M, 2)
            b = video[at].astype(jnp.float32) + mult[at] * (1.0 / MU)
            tile = [b - fore[at], b, dual[0, at], dual[1, at], dual[2, at]]
            tile = [jnp.concatenate([x, row_hi[k, at], row_lo[k, at]], 1) for k, x in enumerate(tile)]
        else:
            side, cor = (col_lo, cor_lo) if e < M else (col_hi, cor_hi)
            at = pl.ds(e if e < M else e - tw - M, 2)
            tile = [jnp.concatenate([side[k, at], cor[0, k, at], cor[1, k, at]], 1) for k in range(5)]
        hi, lo = split(tile[0].reshape(2 * eh, n))
        x2[e * eh : (e + 2) * eh] = jnp.concatenate([hi, lo], 1)
        at = pl.ds(e, 2)
        t_ref[at] = tile[1]
        qf[at] = tile[2] * mask_f
        qh[at] = tile[3] * bound_h
        qw[at] = tile[4]
        for x in (M - 1, tw + M - 1):
            if x in (e, e + 1):
                qw[x] = tile[4][x - e] * bound_w(where_ref, x, tw)

    def between(k, steps):
        if k == WAIT_AT:
            for copy in arrive:
                copy.wait()
        if k >= WAIT_AT:
            span, units = steps - WAIT_AT, ew // 2
            for u in range((k - WAIT_AT) * units // span, (k + 1 - WAIT_AT) * units // span):
                put(2 * u)

    filt = solve(shrink_ref[0], shrink_ref[1], packed[...], between)
    fh, fl = split(filt)
    weights = jnp.concatenate([jnp.concatenate([fh, fl], 1), jnp.concatenate([fh, jnp.zeros_like(fl)], 1)], 0)

    def low_copy(g, part):
        at = pl.ds(g * part, part)
        return pltpu.make_async_copy(low.at[at], low_out.at[at], low_sem.at[g])

    def low_rank(e, size):
        y = jnp.dot(x2[e * eh : (e + size) * eh], weights, preferred_element_type=jnp.float32)
        y = (y[:, :n] + y[:, n:]).reshape(size, eh, n)
        t_ref[e : e + size] = (t_ref[e : e + size] - y) * scale
        return y

    part = tw // low_sem.shape[0]
    low_rank(0, M)
    for g in range(low_sem.shape[0]):
        low[g * part : (g + 1) * part] = low_rank(M + g * part, part)[:, :th]
        low_copy(g, part).start()
    low_rank(tw + M, M)

    N = eh // 8
    sub = iota((8, n), 0)

    def get(ref, e):
        return [ref[e, pl.ds(i, 8, stride=N), :] for i in range(N)]

    def put_at(ref, e, xs):
        for i, x in enumerate(xs):
            ref[e, pl.ds(i, 8, stride=N), :] = x

    row_at, rows = where_ref[0], where_ref[1]
    bounds_h = [None] * N
    for r, edge in ((th - 1, row_at == rows - 1), (eh - 1, row_at == 0)):
        bounds_h[r % N] = jnp.where((sub == r // N) & edge, 0.0, 1.0)

    def clip(x, b):
        return jnp.clip(x, -1.0, 1.0) if b is None else jnp.minimum(jnp.maximum(x, -b), b)

    groups = sem.shape[0]
    group = tw // groups

    def copies(g):
        at, ext = pl.ds(g * group, group), pl.ds(g * group + M, group)
        pairs = [(x.at[at, pl.ds(0, th)], y.at[at]) for x, y in ((fore_res, fore_out), (mult_res, mult_out))]
        pairs += [(q.at[ext, pl.ds(0, th)], dual_out.at[k, at]) for k, q in enumerate((qf, qh, qw))]
        return [pltpu.make_async_copy(src, dst, sem.at[g, i]) for i, (src, dst) in enumerate(pairs)]

    inverse = lam * (1.0 / KAPPA)
    for s in range(TV_STEPS):
        first, last = s == 0, s == TV_STEPS - 1

        def field(e, f, h, w, w_prev):
            out = []
            for i, t in enumerate(get(t_ref, e)):
                before = h[i - 1] if i else pltpu.roll(h[-1], 1, 0)
                if first and i == (th + M) % N:
                    before = jnp.where(sub == (th + M) // N, 0.0, before)
                out.append(t - KAPPA * ((f[i] - pltpu.roll(f[i], 1, 1)) + (h[i] - before) + (w[i] - w_prev[i])))
            return out

        def body(e, carry):
            f, h, w, v, w_done = carry
            f1, h1, w1 = get(qf, e + 1), get(qh, e + 1), get(qw, e + 1)
            v1 = field(e + 1, f1, h1, w1, w)
            f = [clip(x + (pltpu.roll(y, n - 1, 1) - y), mask_f) for x, y in zip(f, v)]
            after = v[1:] + [pltpu.roll(v[0], 7, 0)]
            h = [clip(x + (z - y), b) for x, y, z, b in zip(h, v, after, bounds_h)]
            w = [jnp.clip(x + (z - y), -1.0, 1.0) for x, y, z in zip(w, v, v1)]
            if last:
                bw = bound_w(where_ref, e, tw)
                t = get(t_ref, e)
                fore_of, mult_of = [], []
                for i in range(N):
                    now = w[i] * bw
                    before = h[i - 1] if i else pltpu.roll(h[-1], 1, 0)
                    lift = ((f[i] - pltpu.roll(f[i], 1, 1)) + (h[i] - before) + (now - w_done[i])) * lam
                    fore_of.append(t[i] * inverse - lift)
                    mult_of.append(lift * MU)
                    w_done[i] = now
                put_at(fore_res, e - M, fore_of)
                put_at(mult_res, e - M, mult_of)
            put_at(qf, e, f)
            put_at(qh, e, h)
            put_at(qw, e, w)
            return f1, h1, w1, v1, w_done

        f, h, w = get(qf, s), get(qh, s), get(qw, s)
        none = [jnp.zeros((8, n), jnp.float32)] * N
        v = field(s, f, h, w, none if first else get(qw, s - 1))
        if not last:
            carry = (f, h, w, v, [])
            start, stop = s, ew - 1 - s
            for _ in range((stop - start) % UNROLL):
                carry = body(start, carry)
                start += 1
            lax.fori_loop(start, stop, body, carry, unroll=UNROLL)
            for e in (M - 1, tw + M - 1):
                qw[e] = qw[e] * bound_w(where_ref, e, tw)
        else:
            f1, h1, w1 = get(qf, s + 1), get(qh, s + 1), get(qw, s + 1)
            v1 = field(s + 1, f1, h1, w1, w)
            bw = bound_w(where_ref, s, tw)
            w_done = [jnp.clip(x + (z - y), -1.0, 1.0) * bw for x, y, z in zip(w, v, v1)]
            carry = (f1, h1, w1, v1, w_done)
            for g in range(groups):
                carry = lax.fori_loop(M + g * group, M + (g + 1) * group, body, carry, unroll=UNROLL_LAST)
                at, ext = pl.ds(g * group, group), pl.ds(g * group + M, group)
                qf[ext, :th] = jnp.where(mask_f > 0.0, qf[ext, :th], dual[0, at])

                @pl.when(where_ref[0] == where_ref[1] - 1)
                def _():
                    qh[ext, th - 1 : th] = dual[1, at, th - 1 : th]

                if g == groups - 1:

                    @pl.when(where_ref[2] == where_ref[3] - 1)
                    def _():
                        qw[tw + M - 1, :th] = dual[2, tw - 1]

                for copy in copies(g):
                    copy.start()
    for g in range(low_sem.shape[0]):
        low_copy(g, part).wait()
    for g in range(groups):
        for copy in copies(g):
            copy.wait()


def tv(where, shrink, lam, packed, video, *arrays):
    tw, th, n = video.shape
    ew, eh = tw + 2 * M, th + 2 * M
    inputs = [pltpu.VMEM(x.shape, x.dtype) for x in (video,) + arrays]
    return call(
        tv_kernel,
        (f32(tw, th, n),) * 3 + (f32(3, tw, th, n),),
        TV_LIMIT,
        [SMEM] * 3 + [VMEM] + [ANY] * len(inputs),
        (ANY,) * 4,
        inputs
        + [pltpu.VMEM((ew * eh, 2 * n), jnp.bfloat16)]
        + [pltpu.VMEM((ew, eh, n), jnp.float32)] * 4
        + [pltpu.VMEM((tw, eh, n), jnp.float32)] * 2
        + [pltpu.VMEM((tw, th, n), jnp.float32)]
        + [pltpu.SemaphoreType.DMA((len(inputs),)), pltpu.SemaphoreType.DMA((GROUPS, 5)), pltpu.SemaphoreType.DMA((3,))],
        flops=1 << 30,
    )(where, shrink, lam, packed, video, *arrays)


def local(video, fore_prev, mult, dual_tv, shrink, tv_weight):
    rows, cols = lax.axis_size("rows"), lax.axis_size("cols")
    up = lambda n: [(i, i + 1) for i in range(n - 1)]
    down = lambda n: [(i + 1, i) for i in range(n - 1)]
    where = jnp.stack([lax.axis_index("rows"), rows, lax.axis_index("cols"), cols]).astype(jnp.int32)
    gram, row_lo, row_hi, col_lo, col_hi = make_gram(tv_weight, video, fore_prev, mult, dual_tv)
    row_lo = lax.ppermute(row_lo, "rows", up(rows))
    row_hi = lax.ppermute(row_hi, "rows", down(rows))
    col_lo = lax.ppermute(col_lo, "cols", up(cols))
    col_hi = lax.ppermute(col_hi, "cols", down(cols))
    cor_lo, cor_hi = corners(row_lo, row_hi)
    cor_lo = lax.ppermute(cor_lo, "cols", up(cols))
    cor_hi = lax.ppermute(cor_hi, "cols", down(cols))
    for axis, to in reduction_rounds(rows, cols):
        gram = gram + lax.ppermute(gram, axis, list(enumerate(to)))
    halos = (row_lo, row_hi, col_lo, col_hi, cor_lo, cor_hi)
    return tv(where, shrink, tv_weight, gram, video, fore_prev, mult, dual_tv, *halos)


def solution(mesh):
    tile = P("cols", "rows", None)
    duals = P(None, "cols", "rows", None)
    return jax.shard_map(
        local,
        mesh=mesh,
        in_specs=(tile, tile, tile, duals, P(), P()),
        out_specs=(tile, tile, tile, duals),
        check_vma=False,
    )
```

```python
import jax
import jax.numpy as jnp
from jax import lax
from jax.experimental import pallas as pl
from jax.experimental.pallas import tpu as pltpu
from jax.sharding import PartitionSpec as P


TV_STEPS = 4
MU = 1.25
KAPPA = 0.08
M = 4
CORES = 2
GROUPS = 6
NY = 4
INTERPRET = False
UNROLL = 11
WAIT_AT = 24
TV_LIMIT = 53
GRAM_LIMIT = 63
CORNER_LIMIT = 40
UNROLL_LAST = 10


def ring_rounds(n):
    if n == 1:
        return []
    if n == 2:
        return [[1, 0]]
    even = [i ^ 1 for i in range(n)]
    odd = [(i + 1) % n if i % 2 else (i - 1) % n for i in range(n)]
    if n == 4:
        return [even, odd]
    assert n == 8
    return [even, odd, [3, 6, 5, 0, 7, 2, 1, 4]]


def reduction_rounds(rows, cols):
    nx, nz = rows // CORES, cols // NY
    out = [("rows", [r ^ 1 for r in range(rows)])]
    for to in ring_rounds(NY):
        out.append(("cols", [c // NY * NY + to[c % NY] for c in range(cols)]))
    for to in ring_rounds(nz):
        out.append(("cols", [to[c // NY] * NY + c % NY for c in range(cols)]))
    for to in ring_rounds(nx):
        out.append(("rows", [to[r // CORES] * CORES + r % CORES for r in range(rows)]))
    return out


def iota(shape, dim):
    return lax.broadcasted_iota(jnp.int32, shape, dim)


def split(x):
    hi = x.astype(jnp.bfloat16)
    return hi, (x - hi.astype(jnp.float32)).astype(jnp.bfloat16)


VMEM = pl.BlockSpec(memory_space=pltpu.VMEM)
SMEM = pl.BlockSpec(memory_space=pltpu.SMEM)
ANY = pl.BlockSpec(memory_space=pl.ANY)


def f32(*shape):
    return jax.ShapeDtypeStruct(shape, jnp.float32)


def call(kernel, outs, limit, ins, out_specs=None, scratch=(), flops=0):
    return pl.pallas_call(
        kernel,
        out_shape=outs,
        in_specs=ins,
        out_specs=out_specs or (VMEM,) * len(outs),
        scratch_shapes=scratch,
        compiler_params=pltpu.CompilerParams(vmem_limit_bytes=int(limit * 2**20)),
        cost_estimate=pl.CostEstimate(flops=flops, bytes_accessed=1 << 20, transcendentals=0),
        interpret=INTERPRET,
    )


def lane_of(n, ref):
    return jnp.where(iota((1, n), 1) < n // 2, ref[0], ref[1])


def gram_kernel(
    lam_ref, video_hbm, fore_hbm, mult_hbm, dual_hbm,
    gram, row_lo_out, row_hi_out, col_lo_out, col_hi_out,
    row_lo, row_hi, col_lo, col_hi, video, fore, mult, by_row, by_col, sem, strip_sem, out_sem,
):
    tw, th, n = fore.shape
    half, quarter = n // 2, n // 4
    parts = sem.shape[0]
    step = tw // parts

    def copies(g):
        at = pl.ds(g * step, step)
        pairs = [(video_hbm, video), (fore_hbm, fore), (mult_hbm, mult)]
        return [pltpu.make_async_copy(src.at[at], dst.at[at], sem.at[g, i]) for i, (src, dst) in enumerate(pairs)]

    strips = []
    for side in range(2):
        pairs = [(dual_hbm.at[:, :, pl.ds((0, th - 8)[side], 8)], by_row.at[side])]
        pairs += [(dual_hbm.at[:, pl.ds((0, tw - 8)[side], 8)], by_col.at[side])]
        strips += [pltpu.make_async_copy(x, y, strip_sem.at[side, i]) for i, (x, y) in enumerate(pairs)]
    for g in range(parts):
        for copy in copies(g):
            copy.start()
    for copy in strips:
        copy.start()
    leave = []

    def send(k):
        pairs = [(row_lo.at[k], row_lo_out.at[k]), (row_hi.at[k], row_hi_out.at[k])]
        tile = pl.ds(0, th)
        pairs += [(x.at[k, :, tile], y.at[k, :, tile]) for x, y in ((col_lo, col_lo_out), (col_hi, col_hi_out))]
        new = [pltpu.make_async_copy(x, y, out_sem.at[i, k]) for i, (x, y) in enumerate(pairs)]
        for copy in new:
            copy.start()
        leave.extend(new)

    acc = jnp.zeros((n, 2 * n), jnp.float32)
    for g in range(parts):
        for copy in copies(g):
            copy.wait()
        at = pl.ds(g * step, step)
        b = video[at].astype(jnp.float32) + mult[at] * (1.0 / MU)
        d = b - fore[at]
        for k, x in enumerate((d, b)):
            row_hi[k, at] = x[:, :M]
            row_lo[k, at] = x[:, th - M :]
            if g == 0:
                col_hi[k, :, :th] = x[:M]
            if g == parts - 1:
                col_lo[k, :, :th] = x[step - M :]
        hi, lo = split(d.reshape(step * th, n))
        acc += lax.dot_general(
            hi, jnp.concatenate([hi, lo], 1), (((0,), (0,)), ((), ())), preferred_element_type=jnp.float32
        )
    send(0)
    for copy in strips:
        copy.wait()
    for k in range(3):
        row_hi[2 + k] = by_row[0, k, :, :M]
        row_lo[2 + k] = by_row[1, k, :, 8 - M :]
        col_hi[2 + k, :, :th] = by_col[0, k, :M]
        col_lo[2 + k, :, :th] = by_col[1, k, 8 - M :]
        send(2 + k)
    lam = lane_of(n, lam_ref)
    row_lo[1, :, 0:1, :] = row_lo[1, :, 0:1, :] + lam[None] * by_row[1, 1, :, 7 - M : 8 - M]
    col_lo[1, 0, :th] = col_lo[1, 0, :th] + lam * by_col[1, 2, 7 - M]
    send(1)
    i, j = iota((half, n), 0), iota((half, n), 1)
    cross = jnp.where(j < half, acc[:half, n:], acc[half:, n:])
    whole = jnp.where(j < half, acc[:half, :n], acc[half:, :n]) + cross
    whole = whole + jnp.concatenate([cross[:, :half].T, cross[:, half:].T], 1)
    other = pltpu.roll(whole, half, 1)
    packed = jnp.where(i <= j, whole, other)
    diag = jnp.sum(jnp.where(i == j, other, 0.0), 0, keepdims=True)
    gram[:quarter] = jnp.where(j[:quarter] < half, packed[:quarter], pltpu.roll(packed[quarter:], half, 1))
    gram[quarter:] = jnp.broadcast_to(diag, (8, n))
    for copy in leave:
        copy.wait()


def make_gram(lam, video, fore, mult, dual):
    tw, th, n = fore.shape
    full = pltpu.VMEM((tw, th, n), jnp.float32)
    halos = ((5, tw, M, n),) * 2 + ((5, M, th + 2 * M, n),) * 2
    return call(
        gram_kernel,
        (f32(n // 4 + 8, n),) + tuple(f32(*x) for x in halos),
        GRAM_LIMIT,
        [SMEM] + [ANY] * 4,
        (VMEM,) + (ANY,) * 4,
        [pltpu.VMEM(x, jnp.float32) for x in halos]
        + [pltpu.VMEM((tw, th, n), video.dtype), full, full]
        + [pltpu.VMEM((2, 3, tw, 8, n), jnp.float32), pltpu.VMEM((2, 3, 8, th, n), jnp.float32)]
        + [pltpu.SemaphoreType.DMA((5, 3)), pltpu.SemaphoreType.DMA((2, 2)), pltpu.SemaphoreType.DMA((4, 5))],
        flops=1 << 28,
    )(lam, video, fore, mult, dual)


def corner_kernel(row_lo, row_hi, col_lo_in, col_hi_in, col_lo, col_hi, parts, both, in_sem, out_sem):
    tw, th = row_lo.shape[1], col_lo.shape[2] - 2 * M
    arrive = []
    for at, first in enumerate((0, tw - M)):
        for k, x in enumerate((row_hi, row_lo)):
            arrive.append(pltpu.make_async_copy(x.at[:, pl.ds(first, M)], parts.at[at, k], in_sem.at[at, k]))
    for copy in arrive:
        copy.start()
    for copy in arrive:
        copy.wait()
    leave = []
    for at, out in enumerate((col_hi, col_lo)):
        both[at] = jnp.concatenate([parts[at, 0], parts[at, 1]], 2)
        leave.append(pltpu.make_async_copy(both.at[at], out.at[:, :, pl.ds(th, 2 * M)], out_sem.at[at]))
        leave[-1].start()
    for copy in leave:
        copy.wait()


def corners(row_lo, row_hi, col_lo, col_hi):
    n = row_lo.shape[-1]
    return pl.pallas_call(
        corner_kernel,
        out_shape=(f32(*col_lo.shape),) * 2,
        in_specs=[ANY] * 4,
        out_specs=(ANY,) * 2,
        scratch_shapes=[
            pltpu.VMEM((2, 2, 5, M, M, n), jnp.float32),
            pltpu.VMEM((2, 5, M, 2 * M, n), jnp.float32),
            pltpu.SemaphoreType.DMA((2, 2)),
            pltpu.SemaphoreType.DMA((2,)),
        ],
        input_output_aliases={2: 0, 3: 1},
        compiler_params=pltpu.CompilerParams(vmem_limit_bytes=int(CORNER_LIMIT * 2**20)),
        cost_estimate=pl.CostEstimate(flops=1 << 20, bytes_accessed=1 << 20, transcendentals=0),
        interpret=INTERPRET,
        name="corners",
    )(row_lo, row_hi, col_lo, col_hi)


def masks(where_ref, th, n):
    row_at, rows = where_ref[0], where_ref[1]
    lane = iota((1, n), 1)
    mask_f = jnp.where((lane == n // 2 - 1) | (lane == n - 1), 0.0, 1.0)
    ring = iota((th + 2 * M, n), 0)
    none = ((ring == th - 1) & (row_at == rows - 1)) | ((ring == th + 2 * M - 1) & (row_at == 0))
    return mask_f, jnp.where(none, 0.0, 1.0), ring


def bound_w(where_ref, e, tw):
    col_at, cols = where_ref[2], where_ref[3]
    none = ((e == M - 1) & (col_at == 0)) | ((e == tw + M - 1) & (col_at == cols - 1))
    return jnp.where(none, 0.0, 1.0)


def solve(shrink0, shrink1, packed, between):
    n = packed.shape[1]
    half = n // 2
    quarter = half // 2
    top = packed[:quarter]
    p = jnp.concatenate([top, pltpu.roll(top, half, 1)], 0)
    i, j = iota((half, n), 0), iota((half, n), 1)
    t = jnp.concatenate([p[:, :half].T] * 2, 1)
    left = j < half
    jj = jnp.where(left, j, j - half)
    p = jnp.where(left, p, pltpu.roll(p, half, 1))
    diag = packed[quarter : quarter + 1]
    diag = jnp.where(left[:1], diag, pltpu.roll(diag, half, 1))
    on = i == jj
    g = jnp.where(left == (i <= jj), p, t)
    g = jnp.where(on & ~left, diag, g)
    dg = jnp.sum(jnp.where(on, g, 0.0), 0, keepdims=True)
    l1 = left[:1]
    tr0 = jnp.sum(jnp.where(l1, dg, 0.0), 1, keepdims=True)
    tr1 = jnp.sum(jnp.where(l1, 0.0, dg), 1, keepdims=True)
    tau = jnp.where(l1, shrink0 * tr0, shrink1 * tr1) * (1.0 / half)
    a = g + jnp.where(on, tau, 0.0)

    pick = jnp.where(left, 0, half)
    for k in range(half):
        col = jnp.take_along_axis(a, pick + k, axis=1)
        d = col[k : k + 1]
        r = 1.0 / d
        at = jj[:1] == k
        s = jnp.where(at, -r, a[k : k + 1] * r)
        col = jnp.where(i == k, -1.0, col)
        a = jnp.where((i == k) | (jj == k), 0.0, a) - col * s
        between(k, half)
    f = tau * a + jnp.where(on, 1.0, 0.0)
    low = jnp.where(left, f, 0.0)
    return jnp.concatenate([low, f - low], 0)


def tv_kernel(
    where_ref, shrink_ref, lam_ref, packed,
    video_in, fore_in, mult_in, dual_in, row_lo_in, row_hi_in, col_lo_in, col_hi_in,
    low_out, fore_out, mult_out, dual_out,
    video, fore, mult, dual, row_lo, row_hi, col_lo, col_hi,
    x2, t_ref, qf, qh, qw, fore_res, mult_res, low, in_sem, sem, low_sem,
):
    tw, th, n = low.shape
    eh, ew = th + 2 * M, tw + 2 * M
    arrive = [
        pltpu.make_async_copy(src, dst, in_sem.at[i])
        for i, (src, dst) in enumerate(
            zip(
                (video_in, fore_in, mult_in, dual_in, row_lo_in, row_hi_in, col_lo_in, col_hi_in),
                (video, fore, mult, dual, row_lo, row_hi, col_lo, col_hi),
                strict=True,
            )
        )
    ]
    for copy in arrive:
        copy.start()
    lam = lane_of(n, lam_ref)
    scale = KAPPA / lam
    mask_f, bound_h, _ = masks(where_ref, th, n)

    def put(e):
        if M <= e < tw + M:
            at = pl.ds(e - M, 2)
            b = video[at].astype(jnp.float32) + mult[at] * (1.0 / MU)
            tile = [b - fore[at], b, dual[0, at], dual[1, at], dual[2, at]]
            tile = [jnp.concatenate([x, row_hi[k, at], row_lo[k, at]], 1) for k, x in enumerate(tile)]
        else:
            side, at = (col_lo, pl.ds(e, 2)) if e < M else (col_hi, pl.ds(e - tw - M, 2))
            tile = [side[k, at] for k in range(5)]
        hi, lo = split(tile[0].reshape(2 * eh, n))
        x2[e * eh : (e + 2) * eh] = jnp.concatenate([hi, lo], 1)
        at = pl.ds(e, 2)
        t_ref[at] = tile[1]
        qf[at] = tile[2] * mask_f
        qh[at] = tile[3] * bound_h
        qw[at] = tile[4]
        for x in (M - 1, tw + M - 1):
            if x in (e, e + 1):
                qw[x] = tile[4][x - e] * bound_w(where_ref, x, tw)

    def between(k, steps):
        if k == WAIT_AT:
            for copy in arrive:
                copy.wait()
        if k >= WAIT_AT:
            span, units = steps - WAIT_AT, ew // 2
            for u in range((k - WAIT_AT) * units // span, (k + 1 - WAIT_AT) * units // span):
                put(2 * u)

    filt = solve(shrink_ref[0], shrink_ref[1], packed[...], between)
    fh, fl = split(filt)
    weights = jnp.concatenate([jnp.concatenate([fh, fl], 1), jnp.concatenate([fh, jnp.zeros_like(fl)], 1)], 0)

    def low_copy(g, part):
        at = pl.ds(g * part, part)
        return pltpu.make_async_copy(low.at[at], low_out.at[at], low_sem.at[g])

    def low_rank(e, size):
        y = jnp.dot(x2[e * eh : (e + size) * eh], weights, preferred_element_type=jnp.float32)
        y = (y[:, :n] + y[:, n:]).reshape(size, eh, n)
        t_ref[e : e + size] = (t_ref[e : e + size] - y) * scale
        return y

    part = tw // low_sem.shape[0]
    low_rank(0, M)
    for g in range(low_sem.shape[0]):
        low[g * part : (g + 1) * part] = low_rank(M + g * part, part)[:, :th]
        low_copy(g, part).start()
    low_rank(tw + M, M)

    N = eh // 8
    sub = iota((8, n), 0)

    def get(ref, e):
        return [ref[e, pl.ds(i, 8, stride=N), :] for i in range(N)]

    def put_at(ref, e, xs):
        for i, x in enumerate(xs):
            ref[e, pl.ds(i, 8, stride=N), :] = x

    row_at, rows = where_ref[0], where_ref[1]
    bounds_h = [None] * N
    for r, edge in ((th - 1, row_at == rows - 1), (eh - 1, row_at == 0)):
        bounds_h[r % N] = jnp.where((sub == r // N) & edge, 0.0, 1.0)

    def clip(x, b):
        return jnp.clip(x, -1.0, 1.0) if b is None else jnp.minimum(jnp.maximum(x, -b), b)

    groups = sem.shape[0]
    group = tw // groups

    def copies(g):
        at, ext = pl.ds(g * group, group), pl.ds(g * group + M, group)
        pairs = [(x.at[at, pl.ds(0, th)], y.at[at]) for x, y in ((fore_res, fore_out), (mult_res, mult_out))]
        pairs += [(q.at[ext, pl.ds(0, th)], dual_out.at[k, at]) for k, q in enumerate((qf, qh, qw))]
        return [pltpu.make_async_copy(src, dst, sem.at[g, i]) for i, (src, dst) in enumerate(pairs)]

    inverse = lam * (1.0 / KAPPA)
    for s in range(TV_STEPS):
        first, last = s == 0, s == TV_STEPS - 1

        def field(e, f, h, w, w_prev):
            out = []
            for i, t in enumerate(get(t_ref, e)):
                before = h[i - 1] if i else pltpu.roll(h[-1], 1, 0)
                if first and i == (th + M) % N:
                    before = jnp.where(sub == (th + M) // N, 0.0, before)
                out.append(t - KAPPA * ((f[i] - pltpu.roll(f[i], 1, 1)) + (h[i] - before) + (w[i] - w_prev[i])))
            return out

        def body(e, carry):
            f, h, w, v, w_done = carry
            f1, h1, w1 = get(qf, e + 1), get(qh, e + 1), get(qw, e + 1)
            v1 = field(e + 1, f1, h1, w1, w)
            f = [clip(x + (pltpu.roll(y, n - 1, 1) - y), mask_f) for x, y in zip(f, v)]
            after = v[1:] + [pltpu.roll(v[0], 7, 0)]
            h = [clip(x + (z - y), b) for x, y, z, b in zip(h, v, after, bounds_h)]
            w = [jnp.clip(x + (z - y), -1.0, 1.0) for x, y, z in zip(w, v, v1)]
            if last:
                bw = bound_w(where_ref, e, tw)
                t = get(t_ref, e)
                fore_of, mult_of = [], []
                for i in range(N):
                    now = w[i] * bw
                    before = h[i - 1] if i else pltpu.roll(h[-1], 1, 0)
                    lift = ((f[i] - pltpu.roll(f[i], 1, 1)) + (h[i] - before) + (now - w_done[i])) * lam
                    fore_of.append(t[i] * inverse - lift)
                    mult_of.append(lift * MU)
                    w_done[i] = now
                put_at(fore_res, e - M, fore_of)
                put_at(mult_res, e - M, mult_of)
            put_at(qf, e, f)
            put_at(qh, e, h)
            put_at(qw, e, w)
            return f1, h1, w1, v1, w_done

        f, h, w = get(qf, s), get(qh, s), get(qw, s)
        none = [jnp.zeros((8, n), jnp.float32)] * N
        v = field(s, f, h, w, none if first else get(qw, s - 1))
        if not last:
            carry = (f, h, w, v, [])
            start, stop = s, ew - 1 - s
            for _ in range((stop - start) % UNROLL):
                carry = body(start, carry)
                start += 1
            lax.fori_loop(start, stop, body, carry, unroll=UNROLL)
            for e in (M - 1, tw + M - 1):
                qw[e] = qw[e] * bound_w(where_ref, e, tw)
        else:
            f1, h1, w1 = get(qf, s + 1), get(qh, s + 1), get(qw, s + 1)
            v1 = field(s + 1, f1, h1, w1, w)
            bw = bound_w(where_ref, s, tw)
            w_done = [jnp.clip(x + (z - y), -1.0, 1.0) * bw for x, y, z in zip(w, v, v1)]
            carry = (f1, h1, w1, v1, w_done)
            for g in range(groups):
                carry = lax.fori_loop(M + g * group, M + (g + 1) * group, body, carry, unroll=UNROLL_LAST)
                at, ext = pl.ds(g * group, group), pl.ds(g * group + M, group)
                qf[ext, :th] = jnp.where(mask_f > 0.0, qf[ext, :th], dual[0, at])

                @pl.when(where_ref[0] == where_ref[1] - 1)
                def _():
                    qh[ext, th - 1 : th] = dual[1, at, th - 1 : th]

                if g == groups - 1:

                    @pl.when(where_ref[2] == where_ref[3] - 1)
                    def _():
                        qw[tw + M - 1, :th] = dual[2, tw - 1]

                for copy in copies(g):
                    copy.start()
    for g in range(low_sem.shape[0]):
        low_copy(g, part).wait()
    for g in range(groups):
        for copy in copies(g):
            copy.wait()


def tv(where, shrink, lam, packed, video, *arrays):
    tw, th, n = video.shape
    ew, eh = tw + 2 * M, th + 2 * M
    inputs = [pltpu.VMEM(x.shape, x.dtype) for x in (video,) + arrays]
    return call(
        tv_kernel,
        (f32(tw, th, n),) * 3 + (f32(3, tw, th, n),),
        TV_LIMIT,
        [SMEM] * 3 + [VMEM] + [ANY] * len(inputs),
        (ANY,) * 4,
        inputs
        + [pltpu.VMEM((ew * eh, 2 * n), jnp.bfloat16)]
        + [pltpu.VMEM((ew, eh, n), jnp.float32)] * 4
        + [pltpu.VMEM((tw, eh, n), jnp.float32)] * 2
        + [pltpu.VMEM((tw, th, n), jnp.float32)]
        + [pltpu.SemaphoreType.DMA((len(inputs),)), pltpu.SemaphoreType.DMA((GROUPS, 5)), pltpu.SemaphoreType.DMA((3,))],
        flops=1 << 30,
    )(where, shrink, lam, packed, video, *arrays)


def local(video, fore_prev, mult, dual_tv, shrink, tv_weight):
    rows, cols = lax.axis_size("rows"), lax.axis_size("cols")
    up = lambda n: [(i, i + 1) for i in range(n - 1)]
    down = lambda n: [(i + 1, i) for i in range(n - 1)]
    where = jnp.stack([lax.axis_index("rows"), rows, lax.axis_index("cols"), cols]).astype(jnp.int32)
    gram, row_lo, row_hi, col_lo, col_hi = make_gram(tv_weight, video, fore_prev, mult, dual_tv)
    row_lo = lax.ppermute(row_lo, "rows", up(rows))
    row_hi = lax.ppermute(row_hi, "rows", down(rows))
    col_lo, col_hi = corners(row_lo, row_hi, col_lo, col_hi)
    col_lo = lax.ppermute(col_lo, "cols", up(cols))
    col_hi = lax.ppermute(col_hi, "cols", down(cols))
    for axis, to in reduction_rounds(rows, cols):
        gram = gram + lax.ppermute(gram, axis, list(enumerate(to)))
    halos = (row_lo, row_hi, col_lo, col_hi)
    return tv(where, shrink, tv_weight, gram, video, fore_prev, mult, dual_tv, *halos)


def solution(mesh):
    tile = P("cols", "rows", None)
    duals = P(None, "cols", "rows", None)
    return jax.shard_map(
        local,
        mesh=mesh,
        in_specs=(tile, tile, tile, duals, P(), P()),
        out_specs=(tile, tile, tile, duals),
        check_vma=False,
    )
```

```python
import jax
import jax.numpy as jnp
from jax import lax
from jax.experimental import pallas as pl
from jax.experimental.pallas import tpu as pltpu
from jax.sharding import PartitionSpec as P


TV_STEPS = 4
MU = 1.25
KAPPA = 0.08
M = 4
CORES = 2
GROUPS = 6
NY = 4
INTERPRET = False
UNROLL = 11
WAIT_AT = 24
TV_LIMIT = 53
GRAM_LIMIT = 63
CORNER_LIMIT = 40
UNROLL_LAST = 10


def ring_rounds(n):
    if n == 1:
        return []
    if n == 2:
        return [[1, 0]]
    even = [i ^ 1 for i in range(n)]
    odd = [(i + 1) % n if i % 2 else (i - 1) % n for i in range(n)]
    if n == 4:
        return [even, odd]
    assert n == 8
    return [even, odd, [3, 6, 5, 0, 7, 2, 1, 4]]


def reduction_rounds(rows, cols):
    nx, nz = rows // CORES, cols // NY
    out = [("rows", [r ^ 1 for r in range(rows)])]
    for to in ring_rounds(NY):
        out.append(("cols", [c // NY * NY + to[c % NY] for c in range(cols)]))
    for to in ring_rounds(nz):
        out.append(("cols", [to[c // NY] * NY + c % NY for c in range(cols)]))
    for to in ring_rounds(nx):
        out.append(("rows", [to[r // CORES] * CORES + r % CORES for r in range(rows)]))
    return out


def iota(shape, dim):
    return lax.broadcasted_iota(jnp.int32, shape, dim)


def split(x):
    hi = x.astype(jnp.bfloat16)
    return hi, (x - hi.astype(jnp.float32)).astype(jnp.bfloat16)


VMEM = pl.BlockSpec(memory_space=pltpu.VMEM)
SMEM = pl.BlockSpec(memory_space=pltpu.SMEM)
ANY = pl.BlockSpec(memory_space=pl.ANY)


def f32(*shape):
    return jax.ShapeDtypeStruct(shape, jnp.float32)


def call(kernel, outs, limit, ins, out_specs=None, scratch=(), flops=0):
    return pl.pallas_call(
        kernel,
        out_shape=outs,
        in_specs=ins,
        out_specs=out_specs or (VMEM,) * len(outs),
        scratch_shapes=scratch,
        compiler_params=pltpu.CompilerParams(vmem_limit_bytes=int(limit * 2**20)),
        cost_estimate=pl.CostEstimate(flops=flops, bytes_accessed=1 << 20, transcendentals=0),
        interpret=INTERPRET,
    )


def lane_of(n, ref):
    return jnp.where(iota((1, n), 1) < n // 2, ref[0], ref[1])


def gram_kernel(
    lam_ref, video_hbm, fore_hbm, mult_hbm, dual_hbm,
    gram, row_lo_out, row_hi_out, col_lo_out, col_hi_out,
    row_lo, row_hi, col_lo, col_hi, video, fore, mult, by_row, by_col, sem, strip_sem, out_sem,
):
    tw, th, n = fore.shape
    half, quarter = n // 2, n // 4
    parts = sem.shape[0]
    step = tw // parts

    def copies(g):
        at = pl.ds(g * step, step)
        pairs = [(video_hbm, video), (fore_hbm, fore), (mult_hbm, mult)]
        return [pltpu.make_async_copy(src.at[at], dst.at[at], sem.at[g, i]) for i, (src, dst) in enumerate(pairs)]

    strips = []
    for side in range(2):
        pairs = [(dual_hbm.at[:, :, pl.ds((0, th - 8)[side], 8)], by_row.at[side])]
        pairs += [(dual_hbm.at[:, pl.ds((0, tw - 8)[side], 8)], by_col.at[side])]
        strips += [pltpu.make_async_copy(x, y, strip_sem.at[side, i]) for i, (x, y) in enumerate(pairs)]
    for g in range(parts):
        for copy in copies(g):
            copy.start()
    for copy in strips:
        copy.start()
    leave = []

    def send(k):
        pairs = [(row_lo.at[k], row_lo_out.at[k]), (row_hi.at[k], row_hi_out.at[k])]
        tile = pl.ds(0, th)
        pairs += [(x.at[k, :, tile], y.at[k, :, tile]) for x, y in ((col_lo, col_lo_out), (col_hi, col_hi_out))]
        new = [pltpu.make_async_copy(x, y, out_sem.at[i, k]) for i, (x, y) in enumerate(pairs)]
        for copy in new:
            copy.start()
        leave.extend(new)

    acc = jnp.zeros((n, 2 * n), jnp.float32)
    for g in range(parts):
        for copy in copies(g):
            copy.wait()
        at = pl.ds(g * step, step)
        b = video[at].astype(jnp.float32) + mult[at] * (1.0 / MU)
        d = b - fore[at]
        for k, x in enumerate((d, b)):
            row_hi[k, at] = x[:, :M]
            row_lo[k, at] = x[:, th - M :]
            if g == 0:
                col_hi[k, :, :th] = x[:M]
            if g == parts - 1:
                col_lo[k, :, :th] = x[step - M :]
        hi, lo = split(d.reshape(step * th, n))
        acc += lax.dot_general(
            hi, jnp.concatenate([hi, lo], 1), (((0,), (0,)), ((), ())), preferred_element_type=jnp.float32
        )
    send(0)
    for copy in strips:
        copy.wait()
    for k in range(3):
        row_hi[2 + k] = by_row[0, k, :, :M]
        row_lo[2 + k] = by_row[1, k, :, 8 - M :]
        col_hi[2 + k, :, :th] = by_col[0, k, :M]
        col_lo[2 + k, :, :th] = by_col[1, k, 8 - M :]
        send(2 + k)
    lam = lane_of(n, lam_ref)
    row_lo[1, :, 0:1, :] = row_lo[1, :, 0:1, :] + lam[None] * by_row[1, 1, :, 7 - M : 8 - M]
    col_lo[1, 0, :th] = col_lo[1, 0, :th] + lam * by_col[1, 2, 7 - M]
    send(1)
    i, j = iota((half, n), 0), iota((half, n), 1)
    cross = jnp.where(j < half, acc[:half, n:], acc[half:, n:])
    whole = jnp.where(j < half, acc[:half, :n], acc[half:, :n]) + cross
    whole = whole + jnp.concatenate([cross[:, :half].T, cross[:, half:].T], 1)
    other = pltpu.roll(whole, half, 1)
    packed = jnp.where(i <= j, whole, other)
    diag = jnp.sum(jnp.where(i == j, other, 0.0), 0, keepdims=True)
    gram[:quarter] = jnp.where(j[:quarter] < half, packed[:quarter], pltpu.roll(packed[quarter:], half, 1))
    gram[quarter:] = jnp.broadcast_to(diag, (8, n))
    for copy in leave:
        copy.wait()


def make_gram(lam, video, fore, mult, dual):
    tw, th, n = fore.shape
    full = pltpu.VMEM((tw, th, n), jnp.float32)
    halos = ((5, tw, M, n),) * 2 + ((5, M, th + 2 * M, n),) * 2
    return call(
        gram_kernel,
        (f32(n // 4 + 8, n),) + tuple(f32(*x) for x in halos),
        GRAM_LIMIT,
        [SMEM] + [ANY] * 4,
        (VMEM,) + (ANY,) * 4,
        [pltpu.VMEM(x, jnp.float32) for x in halos]
        + [pltpu.VMEM((tw, th, n), video.dtype), full, full]
        + [pltpu.VMEM((2, 3, tw, 8, n), jnp.float32), pltpu.VMEM((2, 3, 8, th, n), jnp.float32)]
        + [pltpu.SemaphoreType.DMA((5, 3)), pltpu.SemaphoreType.DMA((2, 2)), pltpu.SemaphoreType.DMA((4, 5))],
        flops=1 << 28,
    )(lam, video, fore, mult, dual)


def corner_kernel(row_lo, row_hi, col_lo_in, col_hi_in, col_lo, col_hi, parts, both, in_sem, out_sem):
    tw, th = row_lo.shape[1], col_lo.shape[2] - 2 * M
    arrive = []
    for at, first in enumerate((0, tw - M)):
        for k, x in enumerate((row_hi, row_lo)):
            arrive.append(pltpu.make_async_copy(x.at[:, pl.ds(first, M)], parts.at[at, k], in_sem.at[at, k]))
    for copy in arrive:
        copy.start()
    for copy in arrive:
        copy.wait()
    leave = []
    for at, out in enumerate((col_hi, col_lo)):
        both[at] = jnp.concatenate([parts[at, 0], parts[at, 1]], 2)
        leave.append(pltpu.make_async_copy(both.at[at], out.at[:, :, pl.ds(th, 2 * M)], out_sem.at[at]))
        leave[-1].start()
    for copy in leave:
        copy.wait()


def corners(row_lo, row_hi, col_lo, col_hi):
    n = row_lo.shape[-1]
    return pl.pallas_call(
        corner_kernel,
        out_shape=(f32(*col_lo.shape),) * 2,
        in_specs=[ANY] * 4,
        out_specs=(ANY,) * 2,
        scratch_shapes=[
            pltpu.VMEM((2, 2, 5, M, M, n), jnp.float32),
            pltpu.VMEM((2, 5, M, 2 * M, n), jnp.float32),
            pltpu.SemaphoreType.DMA((2, 2)),
            pltpu.SemaphoreType.DMA((2,)),
        ],
        input_output_aliases={2: 0, 3: 1},
        compiler_params=pltpu.CompilerParams(vmem_limit_bytes=int(CORNER_LIMIT * 2**20)),
        cost_estimate=pl.CostEstimate(flops=1 << 20, bytes_accessed=1 << 20, transcendentals=0),
        interpret=INTERPRET,
        name="corners",
    )(row_lo, row_hi, col_lo, col_hi)


def masks(where_ref, th, n):
    row_at, rows = where_ref[0], where_ref[1]
    lane = iota((1, n), 1)
    mask_f = jnp.where((lane == n // 2 - 1) | (lane == n - 1), 0.0, 1.0)
    ring = iota((th + 2 * M, n), 0)
    none = ((ring == th - 1) & (row_at == rows - 1)) | ((ring == th + 2 * M - 1) & (row_at == 0))
    return mask_f, jnp.where(none, 0.0, 1.0), ring


def bound_w(where_ref, e, tw):
    col_at, cols = where_ref[2], where_ref[3]
    none = ((e == M - 1) & (col_at == 0)) | ((e == tw + M - 1) & (col_at == cols - 1))
    return jnp.where(none, 0.0, 1.0)


def solve(shrink0, shrink1, packed, between):
    n = packed.shape[1]
    half = n // 2
    quarter = half // 2
    top = packed[:quarter]
    p = jnp.concatenate([top, pltpu.roll(top, half, 1)], 0)
    i, j = iota((half, n), 0), iota((half, n), 1)
    t = jnp.concatenate([p[:, :half].T] * 2, 1)
    left = j < half
    jj = jnp.where(left, j, j - half)
    p = jnp.where(left, p, pltpu.roll(p, half, 1))
    diag = packed[quarter : quarter + 1]
    diag = jnp.where(left[:1], diag, pltpu.roll(diag, half, 1))
    on = i == jj
    g = jnp.where(left == (i <= jj), p, t)
    g = jnp.where(on & ~left, diag, g)
    dg = jnp.sum(jnp.where(on, g, 0.0), 0, keepdims=True)
    l1 = left[:1]
    tr0 = jnp.sum(jnp.where(l1, dg, 0.0), 1, keepdims=True)
    tr1 = jnp.sum(jnp.where(l1, 0.0, dg), 1, keepdims=True)
    tau = jnp.where(l1, shrink0 * tr0, shrink1 * tr1) * (1.0 / half)
    a = g + jnp.where(on, tau, 0.0)

    pick = jnp.where(left, 0, half)
    for k in range(0, half, 2):
        c0 = jnp.take_along_axis(a, pick + k, axis=1)
        c1 = jnp.take_along_axis(a, pick + (k + 1), axis=1)
        r0, r1 = a[k : k + 1], a[k + 1 : k + 2]
        p, q, d = c0[k : k + 1], c0[k + 1 : k + 2], c1[k + 1 : k + 2]
        rp = 1.0 / p
        m = q * rp
        i11 = 1.0 / (d - q * m)
        i01 = -m * i11
        i00 = rp - m * i01
        at0, at1 = jj[:1] == k, jj[:1] == k + 1
        s0 = jnp.where(at0, -i00, jnp.where(at1, -i01, i00 * r0 + i01 * r1))
        s1 = jnp.where(at0, -i01, jnp.where(at1, -i11, i01 * r0 + i11 * r1))
        in0, in1 = i == k, i == k + 1
        c0 = jnp.where(in0, -1.0, jnp.where(in1, 0.0, c0))
        c1 = jnp.where(in1, -1.0, jnp.where(in0, 0.0, c1))
        keep = jnp.where(in0 | in1 | (jj == k) | (jj == k + 1), 0.0, a)
        a = keep - c0 * s0 - c1 * s1
        between(k, half)
        between(k + 1, half)
    f = tau * a + jnp.where(on, 1.0, 0.0)
    low = jnp.where(left, f, 0.0)
    return jnp.concatenate([low, f - low], 0)


def tv_kernel(
    where_ref, shrink_ref, lam_ref, packed,
    video_in, fore_in, mult_in, dual_in, row_lo_in, row_hi_in, col_lo_in, col_hi_in,
    low_out, fore_out, mult_out, dual_out,
    video, fore, mult, dual, row_lo, row_hi, col_lo, col_hi,
    x2, t_ref, qf, qh, qw, fore_res, mult_res, low, in_sem, sem, low_sem,
):
    tw, th, n = low.shape
    eh, ew = th + 2 * M, tw + 2 * M
    arrive = [
        pltpu.make_async_copy(src, dst, in_sem.at[i])
        for i, (src, dst) in enumerate(
            zip(
                (video_in, fore_in, mult_in, dual_in, row_lo_in, row_hi_in, col_lo_in, col_hi_in),
                (video, fore, mult, dual, row_lo, row_hi, col_lo, col_hi),
                strict=True,
            )
        )
    ]
    for copy in arrive:
        copy.start()
    lam = lane_of(n, lam_ref)
    scale = KAPPA / lam
    mask_f, bound_h, _ = masks(where_ref, th, n)

    def put(e):
        if M <= e < tw + M:
            at = pl.ds(e - M, 2)
            b = video[at].astype(jnp.float32) + mult[at] * (1.0 / MU)
            tile = [b - fore[at], b, dual[0, at], dual[1, at], dual[2, at]]
            tile = [jnp.concatenate([x, row_hi[k, at], row_lo[k, at]], 1) for k, x in enumerate(tile)]
        else:
            side, at = (col_lo, pl.ds(e, 2)) if e < M else (col_hi, pl.ds(e - tw - M, 2))
            tile = [side[k, at] for k in range(5)]
        hi, lo = split(tile[0].reshape(2 * eh, n))
        x2[e * eh : (e + 2) * eh] = jnp.concatenate([hi, lo], 1)
        at = pl.ds(e, 2)
        t_ref[at] = tile[1]
        qf[at] = tile[2] * mask_f
        qh[at] = tile[3] * bound_h
        qw[at] = tile[4]
        for x in (M - 1, tw + M - 1):
            if x in (e, e + 1):
                qw[x] = tile[4][x - e] * bound_w(where_ref, x, tw)

    def between(k, steps):
        if k == WAIT_AT:
            for copy in arrive:
                copy.wait()
        if k >= WAIT_AT:
            span, units = steps - WAIT_AT, ew // 2
            for u in range((k - WAIT_AT) * units // span, (k + 1 - WAIT_AT) * units // span):
                put(2 * u)

    filt = solve(shrink_ref[0], shrink_ref[1], packed[...], between)
    fh, fl = split(filt)
    weights = jnp.concatenate([jnp.concatenate([fh, fl], 1), jnp.concatenate([fh, jnp.zeros_like(fl)], 1)], 0)

    def low_copy(g, part):
        at = pl.ds(g * part, part)
        return pltpu.make_async_copy(low.at[at], low_out.at[at], low_sem.at[g])

    def low_rank(e, size):
        y = jnp.dot(x2[e * eh : (e + size) * eh], weights, preferred_element_type=jnp.float32)
        y = (y[:, :n] + y[:, n:]).reshape(size, eh, n)
        t_ref[e : e + size] = (t_ref[e : e + size] - y) * scale
        return y

    part = tw // low_sem.shape[0]
    low_rank(0, M)
    for g in range(low_sem.shape[0]):
        low[g * part : (g + 1) * part] = low_rank(M + g * part, part)[:, :th]
        low_copy(g, part).start()
    low_rank(tw + M, M)

    N = eh // 8
    sub = iota((8, n), 0)

    def get(ref, e):
        return [ref[e, pl.ds(i, 8, stride=N), :] for i in range(N)]

    def put_at(ref, e, xs):
        for i, x in enumerate(xs):
            ref[e, pl.ds(i, 8, stride=N), :] = x

    row_at, rows = where_ref[0], where_ref[1]
    bounds_h = [None] * N
    for r, edge in ((th - 1, row_at == rows - 1), (eh - 1, row_at == 0)):
        bounds_h[r % N] = jnp.where((sub == r // N) & edge, 0.0, 1.0)

    def clip(x, b):
        return jnp.clip(x, -1.0, 1.0) if b is None else jnp.minimum(jnp.maximum(x, -b), b)

    groups = sem.shape[0]
    group = tw // groups

    def copies(g):
        at, ext = pl.ds(g * group, group), pl.ds(g * group + M, group)
        pairs = [(x.at[at, pl.ds(0, th)], y.at[at]) for x, y in ((fore_res, fore_out), (mult_res, mult_out))]
        pairs += [(q.at[ext, pl.ds(0, th)], dual_out.at[k, at]) for k, q in enumerate((qf, qh, qw))]
        return [pltpu.make_async_copy(src, dst, sem.at[g, i]) for i, (src, dst) in enumerate(pairs)]

    inverse = lam * (1.0 / KAPPA)
    for s in range(TV_STEPS):
        first, last = s == 0, s == TV_STEPS - 1

        def field(e, f, h, w, w_prev):
            out = []
            for i, t in enumerate(get(t_ref, e)):
                before = h[i - 1] if i else pltpu.roll(h[-1], 1, 0)
                if first and i == (th + M) % N:
                    before = jnp.where(sub == (th + M) // N, 0.0, before)
                out.append(t - KAPPA * ((f[i] - pltpu.roll(f[i], 1, 1)) + (h[i] - before) + (w[i] - w_prev[i])))
            return out

        def body(e, carry):
            f, h, w, v, w_done = carry
            f1, h1, w1 = get(qf, e + 1), get(qh, e + 1), get(qw, e + 1)
            v1 = field(e + 1, f1, h1, w1, w)
            f = [clip(x + (pltpu.roll(y, n - 1, 1) - y), mask_f) for x, y in zip(f, v)]
            after = v[1:] + [pltpu.roll(v[0], 7, 0)]
            h = [clip(x + (z - y), b) for x, y, z, b in zip(h, v, after, bounds_h)]
            w = [jnp.clip(x + (z - y), -1.0, 1.0) for x, y, z in zip(w, v, v1)]
            if last:
                bw = bound_w(where_ref, e, tw)
                t = get(t_ref, e)
                fore_of, mult_of = [], []
                for i in range(N):
                    now = w[i] * bw
                    before = h[i - 1] if i else pltpu.roll(h[-1], 1, 0)
                    lift = ((f[i] - pltpu.roll(f[i], 1, 1)) + (h[i] - before) + (now - w_done[i])) * lam
                    fore_of.append(t[i] * inverse - lift)
                    mult_of.append(lift * MU)
                    w_done[i] = now
                put_at(fore_res, e - M, fore_of)
                put_at(mult_res, e - M, mult_of)
            put_at(qf, e, f)
            put_at(qh, e, h)
            put_at(qw, e, w)
            return f1, h1, w1, v1, w_done

        f, h, w = get(qf, s), get(qh, s), get(qw, s)
        none = [jnp.zeros((8, n), jnp.float32)] * N
        v = field(s, f, h, w, none if first else get(qw, s - 1))
        if not last:
            carry = (f, h, w, v, [])
            start, stop = s, ew - 1 - s
            for _ in range((stop - start) % UNROLL):
                carry = body(start, carry)
                start += 1
            lax.fori_loop(start, stop, body, carry, unroll=UNROLL)
            for e in (M - 1, tw + M - 1):
                qw[e] = qw[e] * bound_w(where_ref, e, tw)
        else:
            f1, h1, w1 = get(qf, s + 1), get(qh, s + 1), get(qw, s + 1)
            v1 = field(s + 1, f1, h1, w1, w)
            bw = bound_w(where_ref, s, tw)
            w_done = [jnp.clip(x + (z - y), -1.0, 1.0) * bw for x, y, z in zip(w, v, v1)]
            carry = (f1, h1, w1, v1, w_done)
            for g in range(groups):
                carry = lax.fori_loop(M + g * group, M + (g + 1) * group, body, carry, unroll=UNROLL_LAST)
                at, ext = pl.ds(g * group, group), pl.ds(g * group + M, group)
                qf[ext, :th] = jnp.where(mask_f > 0.0, qf[ext, :th], dual[0, at])

                @pl.when(where_ref[0] == where_ref[1] - 1)
                def _():
                    qh[ext, th - 1 : th] = dual[1, at, th - 1 : th]

                if g == groups - 1:

                    @pl.when(where_ref[2] == where_ref[3] - 1)
                    def _():
                        qw[tw + M - 1, :th] = dual[2, tw - 1]

                for copy in copies(g):
                    copy.start()
    for g in range(low_sem.shape[0]):
        low_copy(g, part).wait()
    for g in range(groups):
        for copy in copies(g):
            copy.wait()


def tv(where, shrink, lam, packed, video, *arrays):
    tw, th, n = video.shape
    ew, eh = tw + 2 * M, th + 2 * M
    inputs = [pltpu.VMEM(x.shape, x.dtype) for x in (video,) + arrays]
    return call(
        tv_kernel,
        (f32(tw, th, n),) * 3 + (f32(3, tw, th, n),),
        TV_LIMIT,
        [SMEM] * 3 + [VMEM] + [ANY] * len(inputs),
        (ANY,) * 4,
        inputs
        + [pltpu.VMEM((ew * eh, 2 * n), jnp.bfloat16)]
        + [pltpu.VMEM((ew, eh, n), jnp.float32)] * 4
        + [pltpu.VMEM((tw, eh, n), jnp.float32)] * 2
        + [pltpu.VMEM((tw, th, n), jnp.float32)]
        + [pltpu.SemaphoreType.DMA((len(inputs),)), pltpu.SemaphoreType.DMA((GROUPS, 5)), pltpu.SemaphoreType.DMA((3,))],
        flops=1 << 30,
    )(where, shrink, lam, packed, video, *arrays)


def local(video, fore_prev, mult, dual_tv, shrink, tv_weight):
    rows, cols = lax.axis_size("rows"), lax.axis_size("cols")
    up = lambda n: [(i, i + 1) for i in range(n - 1)]
    down = lambda n: [(i + 1, i) for i in range(n - 1)]
    where = jnp.stack([lax.axis_index("rows"), rows, lax.axis_index("cols"), cols]).astype(jnp.int32)
    gram, row_lo, row_hi, col_lo, col_hi = make_gram(tv_weight, video, fore_prev, mult, dual_tv)
    row_lo = lax.ppermute(row_lo, "rows", up(rows))
    row_hi = lax.ppermute(row_hi, "rows", down(rows))
    col_lo, col_hi = corners(row_lo, row_hi, col_lo, col_hi)
    col_lo = lax.ppermute(col_lo, "cols", up(cols))
    col_hi = lax.ppermute(col_hi, "cols", down(cols))
    for axis, to in reduction_rounds(rows, cols):
        gram = gram + lax.ppermute(gram, axis, list(enumerate(to)))
    halos = (row_lo, row_hi, col_lo, col_hi)
    return tv(where, shrink, tv_weight, gram, video, fore_prev, mult, dual_tv, *halos)


def solution(mesh):
    tile = P("cols", "rows", None)
    duals = P(None, "cols", "rows", None)
    return jax.shard_map(
        local,
        mesh=mesh,
        in_specs=(tile, tile, tile, duals, P(), P()),
        out_specs=(tile, tile, tile, duals),
        check_vma=False,
    )
```
